32 devices in a mesh: fsdp: 16 (over z, y, x), replica: 2 (over core).
Axes of the slice: x: 2, y: 2, z: 4, core: 2. Of those that a mesh axis runs over, the one named last changes fastest.
Arguments:
- inputs: bfloat16 [4096, 1024], P(('fsdp', 'replica')), may hold values from -6 to 6
- cotangent: bfloat16 [4096, 1024], P(('fsdp', 'replica')), may hold values from -6 to 6
- attn_gain: bfloat16 [1024], P('fsdp'), may hold values from 0.5 to 1.5
- attn_shift: bfloat16 [1024], P('fsdp'), may hold values from -3 to 3
- qkv_weight: bfloat16 [1024, 3072], P('fsdp'), as said below
- qkv_bias: bfloat16 [3072], P('fsdp'), may hold values from -3 to 3
- proj_weight: bfloat16 [1024, 1024], P('fsdp'), may hold values from -1 to 1
- proj_bias: bfloat16 [1024], P('fsdp'), may hold values from -3 to 3
- mlp_gain: bfloat16 [1024], P('fsdp'), may hold values from 0.5 to 1.5
- mlp_shift: bfloat16 [1024], P('fsdp'), may hold values from -3 to 3
- up_weight: bfloat16 [1024, 4096], P('fsdp'), may hold values from -0.1875 to 0.1875
- up_bias: bfloat16 [4096], P('fsdp'), may hold values from -3 to 3
- down_weight: bfloat16 [4096, 1024], P('fsdp'), may hold values from -0.09375 to 0.09375
- down_bias: bfloat16 [1024], P('fsdp'), may hold values from -3 to 3
Outputs:
- output: bfloat16 [4096, 1024], P(('fsdp', 'replica'))
- grad_inputs: bfloat16 [4096, 1024], P(('fsdp', 'replica'))
- grad_attn_gain: float32 [1024], P('fsdp')
- grad_attn_shift: float32 [1024], P('fsdp')
- grad_qkv_weight: float32 [1024, 3072], P('fsdp')
- grad_qkv_bias: float32 [3072], P('fsdp')
- grad_proj_weight: float32 [1024, 1024], P('fsdp')
- grad_proj_bias: float32 [1024], P('fsdp')
- grad_mlp_gain: float32 [1024], P('fsdp')
- grad_mlp_shift: float32 [1024], P('fsdp')
- grad_up_weight: float32 [1024, 4096], P('fsdp')
- grad_up_bias: float32 [4096], P('fsdp')
- grad_down_weight: float32 [4096, 1024], P('fsdp')
- grad_down_bias: float32 [1024], P('fsdp')
The draws below stay inside these ranges and needn't reach their ends.
Inputs may be any that keep to these rules, and one draw needn't show every extreme that they name: qkv_weight has entries of order 1024^-0.5 times a few; its draw is a scaled normal law.
All inputs are finite; a program needn't handle non-finite values.
Results may differ from the reference program's by a relative error of at most 0.017.
Values may be sent and summed in bfloat16 or wider, within the bound.
A program may use at most 192 MiB of HBM per device.

```python
import math
import jax
import jax.numpy as jnp
from jax import lax

D = 1024
H = 16
ROT = 16
FF = 4096
SEQ = 128
TOKENS = 4096


def draw_qkv_weight(key, part):
    entries = jnp.clip(jax.random.normal(key, (D, 3 * D), jnp.float32), -6.0, 6.0) * D ** (-0.5)
    return entries.astype(jnp.bfloat16)


def steps_of(key, dims, cuts, smallest, high):
    factor_of, own = 1.0, jax.random.fold_in(key, 6)
    for dim, parts in cuts:
        steps = jnp.exp(jax.random.uniform(jax.random.fold_in(own, dim), (parts,), jnp.float32, smallest / len(cuts), high / len(cuts)))
        factor_of = factor_of * jnp.repeat(steps, dims[dim] // parts).reshape([-1 if axis == dim else 1 for axis in range(len(dims))])
    return factor_of


def noise(stream_key, dims, width, reach, split=(), kind=jnp.bfloat16):
    values = jax.random.normal(stream_key, dims, jnp.float32) * width
    if len(split) > 0:
        values = steps_of(stream_key, dims, split, -0.22, 0.18) * values
    return jnp.clip(values, min=-reach, max=reach).astype(kind)


def setup_inputs(seed: int = 0) -> dict:
    keys = jax.random.split(jax.random.key(seed), 15)
    inputs = noise(keys[0], (TOKENS, D), 1.0, 6.0, ((0, 32),))
    cotangent = noise(keys[1], (TOKENS, D), 1.0, 6.0, ((0, 32),))
    attn_gain = jnp.clip(1.0 + 0.1 * jax.random.normal(keys[2], (D,), jnp.float32), 0.5, 1.5).astype(jnp.bfloat16)
    attn_shift = noise(keys[3], (D,), 0.5, 3.0, ((0, 16),))
    qkv_weight = draw_qkv_weight(jax.random.fold_in(keys[14], 71), 0)
    qkv_bias = noise(keys[5], (3 * D,), 0.5, 3.0, ((0, 16),))
    proj_weight = noise(keys[6], (D, D), (D * 4 // SEQ) ** -0.5, 1.0, ((0, 16),))
    proj_bias = noise(keys[7], (D,), 0.5, 3.0, ((0, 16),))
    mlp_gain = jnp.clip(1.0 + 0.1 * jax.random.normal(keys[8], (D,), jnp.float32), 0.5, 1.5).astype(jnp.bfloat16)
    mlp_shift = noise(keys[9], (D,), 0.5, 3.0, ((0, 16),))
    up_weight = noise(keys[10], (D, FF), D ** -0.5, 0.1875, ((0, 16),))
    up_bias = noise(keys[11], (FF,), 0.5, 3.0, ((0, 16),))
    down_weight = noise(keys[12], (FF, D), FF ** -0.5, 0.09375, ((0, 16),))
    down_bias = noise(keys[13], (D,), 0.5, 3.0, ((0, 16),))
    return dict(inputs=inputs, cotangent=cotangent, attn_gain=attn_gain, attn_shift=attn_shift, qkv_weight=qkv_weight, qkv_bias=qkv_bias, proj_weight=proj_weight, proj_bias=proj_bias, mlp_gain=mlp_gain, mlp_shift=mlp_shift, up_weight=up_weight, up_bias=up_bias, down_weight=down_weight, down_bias=down_bias)


EPSILON = 1e-05
THETA = 10000.0
SQRT_HALF = 0.7071067811865476
INV_ROOT_TAU = 0.3989422804014327

def product(pattern, left_side, right_side):
    return jnp.einsum(pattern, left_side.astype(jnp.float32), right_side.astype(jnp.float32))

def normalize(residual, gain_row, shift_row):
    centered = residual - lax.optimization_barrier(jnp.mean(residual, axis=-1, keepdims=True))
    inverse = lax.rsqrt(lax.optimization_barrier(jnp.mean(centered * centered, axis=-1, keepdims=True)) + EPSILON)
    unit_rows = centered * inverse
    return (unit_rows * gain_row + shift_row, unit_rows, inverse)

def normalize_back(upstream, unit_rows, inverse, gain_row):
    scaled = upstream * gain_row
    grad_rows = inverse * (scaled - lax.optimization_barrier(jnp.mean(scaled, axis=-1, keepdims=True)) - unit_rows * lax.optimization_barrier(jnp.mean(scaled * unit_rows, axis=-1, keepdims=True)))
    return (grad_rows, lax.optimization_barrier(jnp.sum(upstream * unit_rows, axis=0)), lax.optimization_barrier(jnp.sum(upstream, axis=0)))

def rotary_tables():
    half_rot = ROT // 2
    frequency = jnp.exp(jnp.arange(half_rot, dtype=jnp.float32) * (-2.0 * math.log(THETA) / ROT))
    angles = jnp.arange(SEQ, dtype=jnp.float32)[:, None] * frequency[None, :]
    return (jnp.cos(angles), jnp.sin(angles))

def rotate(heads_data, cosine_table, sine_table, inverse_turn):
    half_rot = ROT // 2
    first_half = heads_data[..., :half_rot]
    second_half = heads_data[..., half_rot:ROT]
    passive = heads_data[..., ROT:]
    cosine_part = cosine_table[None, :, None, :]
    sine_part = sine_table[None, :, None, :]
    if inverse_turn:
        sine_part = -sine_part
    return jnp.concatenate([first_half * cosine_part - second_half * sine_part, second_half * cosine_part + first_half * sine_part, passive], axis=-1)

def gelu_slope(pre_act):
    return 0.5 * (1.0 + lax.erf(pre_act * SQRT_HALF)) + pre_act * jnp.exp(-0.5 * pre_act * pre_act) * INV_ROOT_TAU

def masked_scores(queries, keys_rot):
    head_dim = queries.shape[-1]
    scores = product('bqhd,bkhd->bhqk', queries, keys_rot) * head_dim ** (-0.5)
    positions = jnp.arange(SEQ)
    causal = positions[:, None] >= positions[None, :]
    return jnp.where(causal[None, None], scores, -jnp.inf)

def forward_pass(inputs, forward_set):
    attn_gain, attn_shift, qkv_weight, qkv_bias, proj_weight, proj_bias, mlp_gain, mlp_shift, up_weight, up_bias, down_weight, down_bias = forward_set
    row_count, features = inputs.shape
    seq_count = row_count // SEQ
    head_dim = features // H
    residual = inputs.astype(jnp.float32)
    normed, attn_unit, attn_inverse = normalize(residual, attn_gain.astype(jnp.float32), attn_shift.astype(jnp.float32))
    attn_in = normed.astype(jnp.bfloat16)
    projected = jnp.dot(attn_in, qkv_weight, preferred_element_type=jnp.float32) + qkv_bias.astype(jnp.float32)
    shaped = projected.reshape(seq_count, SEQ, 3, H, head_dim)
    cosine_table, sine_table = rotary_tables()
    queries = rotate(shaped[:, :, 0], cosine_table, sine_table, False).astype(jnp.bfloat16)
    keys_rot = rotate(shaped[:, :, 1], cosine_table, sine_table, False).astype(jnp.bfloat16)
    values = shaped[:, :, 2].astype(jnp.bfloat16)
    scores = masked_scores(queries, keys_rot)
    peak_score = lax.optimization_barrier(jnp.max(scores, axis=-1, keepdims=True))
    logsum = peak_score + jnp.log(lax.optimization_barrier(jnp.sum(jnp.exp(scores - peak_score), axis=-1, keepdims=True)))
    weights = jnp.exp(scores - logsum).astype(jnp.bfloat16)
    context = product('bhqk,bkhd->bqhd', weights, values).reshape(row_count, features).astype(jnp.bfloat16)
    attn_out = jnp.dot(context, proj_weight, preferred_element_type=jnp.float32) + proj_bias.astype(jnp.float32)
    normed_mlp, mlp_unit, mlp_inverse = normalize(residual, mlp_gain.astype(jnp.float32), mlp_shift.astype(jnp.float32))
    mlp_in = normed_mlp.astype(jnp.bfloat16)
    pre_act = jnp.dot(mlp_in, up_weight, preferred_element_type=jnp.float32) + up_bias.astype(jnp.float32)
    activated = jax.nn.gelu(pre_act, approximate=False).astype(jnp.bfloat16)
    mlp_out = jnp.dot(activated, down_weight, preferred_element_type=jnp.float32) + down_bias.astype(jnp.float32)
    output = (residual + attn_out + mlp_out).astype(jnp.bfloat16)
    saved = (attn_unit, attn_inverse, attn_in, queries, keys_rot, values, logsum, context, mlp_unit, mlp_inverse, mlp_in, pre_act, activated)
    return (output, saved)

def backward_pass(cotangent, saved, backward_set):
    attn_gain, attn_shift, qkv_weight, qkv_bias, proj_weight, proj_bias, mlp_gain, mlp_shift, up_weight, up_bias, down_weight, down_bias = backward_set
    attn_unit, attn_inverse, attn_in, queries, keys_rot, values, logsum, context, mlp_unit, mlp_inverse, mlp_in, pre_act, activated = saved
    row_count, features = cotangent.shape
    head_dim = features // H
    upstream = cotangent.astype(jnp.float32)
    grad_out_bias = lax.optimization_barrier(jnp.sum(upstream, axis=0))
    grad_down_weight = jnp.dot(activated.T, cotangent, preferred_element_type=jnp.float32)
    grad_pre = jnp.dot(cotangent, down_weight.T, preferred_element_type=jnp.float32) * gelu_slope(pre_act)
    grad_up_bias = lax.optimization_barrier(jnp.sum(grad_pre, axis=0))
    grad_pre_b = grad_pre.astype(jnp.bfloat16)
    grad_up_weight = jnp.dot(mlp_in.T, grad_pre_b, preferred_element_type=jnp.float32)
    grad_mlp_in = jnp.dot(grad_pre_b, up_weight.T, preferred_element_type=jnp.float32)
    grad_proj_weight = jnp.dot(context.T, cotangent, preferred_element_type=jnp.float32)
    grad_context = jnp.dot(cotangent, proj_weight.T, preferred_element_type=jnp.float32).astype(jnp.bfloat16)
    grad_context = grad_context.reshape(queries.shape)
    probs = jnp.exp(masked_scores(queries, keys_rot) - logsum)
    weights = probs.astype(jnp.bfloat16)
    grad_probs = product('bqhd,bkhd->bhqk', grad_context, values)
    grad_values = product('bhqk,bqhd->bkhd', weights, grad_context)
    grad_scores = (probs * (grad_probs - lax.optimization_barrier(jnp.sum(probs * grad_probs, axis=-1, keepdims=True))) * head_dim ** (-0.5)).astype(jnp.bfloat16)
    grad_queries = product('bhqk,bkhd->bqhd', grad_scores, keys_rot)
    grad_keys = product('bhqk,bqhd->bkhd', grad_scores, queries)
    cosine_table, sine_table = rotary_tables()
    grad_projected = jnp.stack([rotate(grad_queries, cosine_table, sine_table, True), rotate(grad_keys, cosine_table, sine_table, True), grad_values], axis=2).reshape(row_count, 3 * features)
    grad_qkv_bias = lax.optimization_barrier(jnp.sum(grad_projected, axis=0))
    grad_projected_b = grad_projected.astype(jnp.bfloat16)
    grad_qkv_weight = jnp.dot(attn_in.T, grad_projected_b, preferred_element_type=jnp.float32)
    grad_attn_in = jnp.dot(grad_projected_b, qkv_weight.T, preferred_element_type=jnp.float32)
    attn_rows, grad_attn_gain, grad_attn_shift = normalize_back(grad_attn_in, attn_unit, attn_inverse, attn_gain.astype(jnp.float32))
    mlp_rows, grad_mlp_gain, grad_mlp_shift = normalize_back(grad_mlp_in, mlp_unit, mlp_inverse, mlp_gain.astype(jnp.float32))
    grad_inputs = (upstream + attn_rows + mlp_rows).astype(jnp.bfloat16)
    gradients = (grad_attn_gain, grad_attn_shift, grad_qkv_weight, grad_qkv_bias, grad_proj_weight, grad_out_bias, grad_mlp_gain, grad_mlp_shift, grad_up_weight, grad_up_bias, grad_down_weight, grad_out_bias)
    return (grad_inputs, gradients)

def reference(inputs, cotangent, attn_gain, attn_shift, qkv_weight, qkv_bias, proj_weight, proj_bias, mlp_gain, mlp_shift, up_weight, up_bias, down_weight, down_bias):
    parameters = (attn_gain, attn_shift, qkv_weight, qkv_bias, proj_weight, proj_bias, mlp_gain, mlp_shift, up_weight, up_bias, down_weight, down_bias)
    block_seqs = math.gcd(TOKENS // SEQ, max(1, 4096 // SEQ))
    block_rows = block_seqs * SEQ
    block_count = TOKENS // block_rows
    input_blocks = inputs.reshape(block_count, block_rows, D)
    cotangent_blocks = cotangent.reshape(block_count, block_rows, D)
    zero_sums = tuple((jnp.zeros(item.shape, jnp.float32) for item in parameters))

    def accumulate(running, block_pair):
        output_block, saved = forward_pass(block_pair[0], parameters)
        grad_block, gradients = backward_pass(block_pair[1], saved, parameters)
        return (tuple((left_sum + right_sum for left_sum, right_sum in zip(running, gradients))), (output_block, grad_block))
    totals, (outputs, grads_in) = lax.scan(accumulate, zero_sums, (input_blocks, cotangent_blocks))
    return (outputs.reshape(TOKENS, D), grads_in.reshape(TOKENS, D), totals[0], totals[1], totals[2], totals[3], totals[4], totals[5], totals[6], totals[7], totals[8], totals[9], totals[10], totals[11])
```

```python
import functools
import math

import jax
import jax.numpy as jnp
from jax import lax
from jax.experimental import pallas as pl
from jax.experimental.pallas import tpu as pltpu
from jax.sharding import PartitionSpec as P

H = 16
ROT = 16
SEQ = 128


EPSILON = 1e-05
THETA = 10000.0
SQRT_HALF = 0.7071067811865476
INV_ROOT_TAU = 0.3989422804014327


def product(pattern, left_side, right_side):
    return jnp.einsum(pattern, left_side, right_side, preferred_element_type=jnp.float32)


def normalize(residual, gain_row, shift_row):
    centered = residual - jnp.mean(residual, axis=-1, keepdims=True)
    inverse = lax.rsqrt(jnp.mean(centered * centered, axis=-1, keepdims=True) + EPSILON)
    unit_rows = centered * inverse
    return (unit_rows * gain_row + shift_row, unit_rows, inverse)


def normalize_back(upstream, unit_rows, inverse, gain_row):
    scaled = upstream * gain_row
    grad_rows = inverse * (
        scaled
        - jnp.mean(scaled, axis=-1, keepdims=True)
        - unit_rows * jnp.mean(scaled * unit_rows, axis=-1, keepdims=True)
    )
    return (grad_rows, jnp.sum(upstream * unit_rows, axis=0), jnp.sum(upstream, axis=0))


def rotary_tables():
    half_rot = ROT // 2
    frequency = jnp.exp(jnp.arange(half_rot, dtype=jnp.float32) * (-2.0 * math.log(THETA) / ROT))
    angles = jnp.arange(SEQ, dtype=jnp.float32)[:, None] * frequency[None, :]
    return (jnp.cos(angles), jnp.sin(angles))


def rotate(heads_data, cosine_table, sine_table, inverse_turn):
    half_rot = ROT // 2
    first_half = heads_data[..., :half_rot]
    second_half = heads_data[..., half_rot:ROT]
    passive = heads_data[..., ROT:]
    cosine_part = cosine_table[None, :, None, :]
    sine_part = sine_table[None, :, None, :]
    if inverse_turn:
        sine_part = -sine_part
    return jnp.concatenate(
        [
            first_half * cosine_part - second_half * sine_part,
            second_half * cosine_part + first_half * sine_part,
            passive,
        ],
        axis=-1,
    )


def gelu_slope(pre_act):
    return (
        0.5 * (1.0 + lax.erf(pre_act * SQRT_HALF))
        + pre_act * jnp.exp(-0.5 * pre_act * pre_act) * INV_ROOT_TAU
    )


def masked_scores(queries, keys_rot):
    head_dim = queries.shape[-1]
    scores = product("bqhd,bkhd->bhqk", queries, keys_rot) * head_dim ** (-0.5)
    positions = jnp.arange(SEQ)
    causal = positions[:, None] >= positions[None, :]
    return jnp.where(causal[None, None], scores, -jnp.inf)


MESH = pl.DeviceIdType.MESH
LANES = 128
BF16 = jnp.bfloat16
F32 = jnp.float32


def degrees(owners, features):
    line = math.gcd(owners, features // (2 * LANES))
    return line, owners // line


class Place:
    def __init__(self, line, plane):
        self.line, self.plane = line, plane
        owner = lax.axis_index("fsdp")
        replica = lax.axis_index("replica")
        self.t = lax.div(owner, plane)
        self.i = lax.rem(owner, plane)
        self.c = lax.rem(replica, 2)
        self.base = replica - self.c

    def at(self, t, i, c):
        return (t * self.plane + i, self.base + c)

    def on_line(self, k):
        return lax.rem(self.t + (k + self.line), self.line)

    def in_plane(self, k):
        return lax.rem(self.i + (k + self.plane), self.plane)

    def greet(self):
        barrier = pltpu.get_barrier_semaphore()
        peers = [self.at(self.on_line(k), self.i, self.c) for k in range(1, self.line)]
        peers += [self.at(self.t, self.in_plane(k), self.c) for k in range(1, self.plane)]
        peers += [self.at(self.t, self.in_plane(k), 1 - self.c) for k in range(self.plane)]
        for peer in peers:
            pl.semaphore_signal(barrier, inc=1, device_id=peer, device_id_type=MESH)
        pl.semaphore_wait(barrier, len(peers))


class Copies:
    def __init__(self, send, recv):
        self.send, self.recv = send, recv
        self.used = 0
        self.sent = []

    def slots(self, count):
        first = self.used
        self.used += count
        return first

    def push(self, src, dst, peer, slot=None, land=None):
        slot = self.slots(1) if slot is None else slot
        copy = pltpu.make_async_remote_copy(
            src_ref=src,
            dst_ref=dst,
            send_sem=self.send.at[slot],
            recv_sem=self.recv.at[slot if land is None else land],
            device_id=peer,
            device_id_type=MESH,
        )
        copy.start()
        self.sent.append(copy)
        return copy

    def local(self, src, dst, slot=None):
        slot = self.slots(1) if slot is None else slot
        copy = pltpu.make_async_copy(src, dst, self.recv.at[slot])
        copy.start()
        return copy

    def finish(self):
        for copy in self.sent:
            copy.wait_send()


def gather_kernel(
    line, plane, x, cot, wqkv, wproj, wup, wdown, x_all, cot_all, q_part, p_part, u_part, d_part, send, recv
):
    me = Place(line, plane)
    t, i, c = me.t, me.i, me.c
    net = Copies(send, recv)
    features = x.shape[1]
    per_head = q_part.shape[-1]
    per_up = u_part.shape[-1]
    me.greet()

    def lanes(start, size):
        return pl.ds(pl.multiple_of(start * size, LANES), size)

    def spread(k):
        to = me.on_line(k)
        pairs = [
            (wqkv.at[:, lanes(part * 2 * line + 2 * to + c, per_head)], q_part.at[part, t, i])
            for part in range(3)
        ]
        pairs.append((wup.at[:, lanes(2 * to + c, per_up)], u_part.at[t, i]))
        if k == 0:
            return [net.local(src, dst) for src, dst in pairs]
        return [net.push(src, dst, me.at(to, i, c)) for src, dst in pairs]

    def tokens(rows, whole):
        copies = {}
        for k in range(1, line):
            copies[k] = net.push(rows, whole.at[2 * t + c], me.at(me.on_line(k), i, c))
        own = net.local(rows, whole.at[2 * t + c])
        other = net.push(rows, whole.at[2 * t + c], me.at(t, i, 1 - c))
        return copies, own, other

    rows_set = []

    def rows_out(mine, whole):
        half = mine.shape[0] // 2
        group = plane // 2
        core = lax.div(i, group)
        land = pl.ds(pl.multiple_of(lax.rem(i, group) * mine.shape[0] + c * half, half), half)
        src = mine.at[pl.ds(pl.multiple_of(c * half, half), half)]
        dst = whole.at[land]
        first = net.slots(2 * plane)
        for k in range(1, plane):
            net.push(
                src, dst, me.at(t, me.in_plane(k), core), slot=net.slots(1), land=first + 2 * k + c
            )
        away = net.slots(1)

        @pl.when(core == c)
        def _():
            pltpu.make_async_copy(src, dst, recv.at[first + c]).start()

        @pl.when(core != c)
        def _():
            pltpu.make_async_remote_copy(
                src_ref=src,
                dst_ref=dst,
                send_sem=send.at[away],
                recv_sem=recv.at[first + c],
                device_id=me.at(t, i, core),
                device_id_type=MESH,
            ).start()

        def wait():
            for k in range(plane):
                source = me.in_plane(-k)

                @pl.when(lax.div(source, group) == c)
                def _():
                    for s in range(2):
                        at = pl.ds(
                            pl.multiple_of(lax.rem(source, group) * mine.shape[0] + s * half, half), half
                        )
                        pltpu.make_async_copy(
                            whole.at[at], whole.at[at], recv.at[first + 2 * k + s]
                        ).wait()

            @pl.when(core != c)
            def _():
                pltpu.make_async_remote_copy(
                    src_ref=src,
                    dst_ref=dst,
                    send_sem=send.at[away],
                    recv_sem=recv.at[first + c],
                    device_id=me.at(t, i, core),
                    device_id_type=MESH,
                ).wait_send()

        rows_set.append(wait)

    columns = {k: spread(k) for k in range(line)}
    x_copies = tokens(x, x_all)
    rows_out(wproj, p_part)
    rows_out(wdown, d_part)
    cot_copies = tokens(cot, cot_all)

    onward = []
    for k in range(line):
        source = me.on_line(-k)
        for copy in columns[k]:
            copy.wait() if k == 0 else copy.wait_recv()
        for j in range(1, plane):
            peer = me.at(t, me.in_plane(j), c)
            for part in range(3):
                ref = q_part.at[part, source, i]
                onward.append(net.push(ref, ref, peer))
            ref = u_part.at[source, i]
            onward.append(net.push(ref, ref, peer))
    for (copies, own, other), whole in ((x_copies, x_all), (cot_copies, cot_all)):
        for k in range(1, line):
            source = me.on_line(-k)
            copies[k].wait_recv()
            ref = whole.at[2 * source + c]
            onward.append(net.push(ref, ref, me.at(t, i, 1 - c)))
        onward.append(other)
        own.wait()
    for copy in onward:
        copy.wait_recv()
    for wait in rows_set:
        wait()
    net.finish()


def scatter_kernel(
    line,
    plane,
    out_part,
    back_part,
    gq,
    gp,
    gu,
    gd,
    out_sum,
    back_sum,
    gq_out,
    gp_out,
    gu_out,
    gd_out,
    rows_in,
    rows_mid,
    rows_end,
    q_in,
    u_in,
    q_mid,
    u_mid,
    q_end,
    u_end,
    p_in,
    d_in,
    send,
    recv,
):
    me = Place(line, plane)
    t, i, c = me.t, me.i, me.c
    net = Copies(send, recv)
    group = plane // 2
    me.greet()

    sums = ((out_part, 0), (back_part, 1))
    first = []
    for part, n in sums:
        for b in range(line):
            first.append(
                net.push(part.at[2 * b + 1 - c], rows_in.at[n, b], me.at(t, i, 1 - c))
            )
    cols = []
    for k in range(1, plane):
        to = me.in_plane(k)
        peer = me.at(t, to, c)
        cols.append(net.push(gq.at[:, :, to], q_in.at[k], peer))
        cols.append(net.push(gu.at[:, to], u_in.at[k], peer))
    row_waits = []

    def rows_back(mine, landing):
        height = mine.shape[0] // group
        half = height // 2
        slot = net.slots(2 * plane)
        for k in range(plane):
            to = me.in_plane(k)

            @pl.when(lax.div(to, group) == c)
            def _():
                for s in range(2):
                    src = mine.at[
                        pl.ds(pl.multiple_of(lax.rem(to, group) * height + s * half, half), half)
                    ]
                    if k == 0:
                        @pl.when(c == s)
                        def _():
                            pltpu.make_async_copy(src, landing.at[k], recv.at[slot + k]).start()

                        @pl.when(c != s)
                        def _():
                            pltpu.make_async_remote_copy(
                                src_ref=src,
                                dst_ref=landing.at[k],
                                send_sem=send.at[slot + 2 * k + s],
                                recv_sem=recv.at[slot + k],
                                device_id=me.at(t, to, s),
                                device_id_type=MESH,
                            ).start()
                    else:
                        pltpu.make_async_remote_copy(
                            src_ref=src,
                            dst_ref=landing.at[k],
                            send_sem=send.at[slot + 2 * k + s],
                            recv_sem=recv.at[slot + k],
                            device_id=me.at(t, to, s),
                            device_id_type=MESH,
                        ).start()

        def wait_recv():
            for k in range(plane):
                pltpu.make_async_copy(landing.at[k], landing.at[k], recv.at[slot + k]).wait()

        def wait_send():
            for k in range(plane):
                to = me.in_plane(k)

                @pl.when(lax.div(to, group) == c)
                def _():
                    for s in range(2):
                        def done():
                            pltpu.make_async_copy(
                                landing.at[k], landing.at[k], send.at[slot + 2 * k + s]
                            ).wait()

                        if k == 0:
                            pl.when(c != s)(done)
                        else:
                            done()

        return wait_recv, wait_send

    p_recv, p_send = rows_back(gp, p_in)
    d_recv, d_send = rows_back(gd, d_in)

    second = []
    for n, (part, _) in enumerate(sums):
        for b in range(line):
            first[n * line + b].wait_recv()
            rows_mid[n, b] = (
                part[2 * b + c].astype(F32) + rows_in[n, b].astype(F32)
            ).astype(BF16)
        for k in range(1, line):
            to = me.on_line(k)
            second.append(net.push(rows_mid.at[n, to], rows_end.at[n, k], me.at(to, i, c)))

    for copy in cols:
        copy.wait_recv()
    for b in range(line):
        for part in range(3):
            total = gq[part, b, i].astype(F32)
            for k in range(1, plane):
                total = total + q_in[k, part, b].astype(F32)
            q_mid[b, part] = total.astype(BF16)
        total = gu[b, i].astype(F32)
        for k in range(1, plane):
            total = total + u_in[k, b].astype(F32)
        u_mid[b] = total.astype(BF16)
    third = []
    for k in range(1, line):
        to = me.on_line(k)
        peer = me.at(to, i, c)
        third.append(net.push(q_mid.at[to], q_end.at[2 * t + c], peer))
        third.append(net.push(u_mid.at[to], u_end.at[2 * t + c], peer))
    q_end[2 * t + c] = q_mid[t]
    u_end[2 * t + c] = u_mid[t]

    def across(source):
        q_ref, u_ref = q_end.at[2 * source + c], u_end.at[2 * source + c]
        return [
            net.push(q_ref, q_ref, me.at(t, i, 1 - c)),
            net.push(u_ref, u_ref, me.at(t, i, 1 - c)),
        ]

    fourth = across(t)

    def rows_total(landing, whole, wait_recv):
        wait_recv()
        half = landing.shape[1]
        total = landing[0].astype(F32)
        for k in range(1, plane):
            total = total + landing[k].astype(F32)
        mine = pl.ds(pl.multiple_of(c * half, half), half)
        whole[mine] = total
        return net.push(whole.at[mine], whole.at[mine], me.at(t, i, 1 - c))

    fourth.append(rows_total(p_in, gp_out, p_recv))
    fourth.append(rows_total(d_in, gd_out, d_recv))

    for copy in second:
        copy.wait_recv()
    for n, out in ((0, out_sum), (1, back_sum)):
        total = rows_mid[n, t].astype(F32)
        for k in range(1, line):
            total = total + rows_end[n, k].astype(F32)
        out[...] = total
    for k in range(1, line):
        third[2 * k - 2].wait_recv()
        third[2 * k - 1].wait_recv()
        fourth += across(me.on_line(-k))
    for copy in fourth:
        copy.wait_recv()
    per_head = q_end.shape[-1]
    per_up = u_end.shape[-1]
    for b in range(2 * line):
        for part in range(3):
            at = (part * 2 * line + b) * per_head
            gq_out[:, at : at + per_head] = q_end[b, part].astype(F32)
        gu_out[:, b * per_up : (b + 1) * per_up] = u_end[b].astype(F32)
    net.finish()
    p_send()
    d_send()


def shape(dims, kind):
    return jax.ShapeDtypeStruct(dims, kind)


def gather(line, plane, x, cot, wqkv, wproj, wup, wdown):
    rows, features = x.shape
    owners = line * plane
    cores = 2 * line
    own = features // owners
    hidden = wup.shape[1]
    outs = (
        shape((cores, rows, features), BF16),
        shape((cores, rows, features), BF16),
        shape((3, line, plane, own, features // cores), BF16),
        shape((features // cores, features), BF16),
        shape((line, plane, own, hidden // cores), BF16),
        shape((hidden // cores, features), BF16),
    )
    sems = 8 * line + 4 * line * plane + 12 * plane + 64
    return pl.pallas_call(
        functools.partial(gather_kernel, line, plane),
        out_shape=outs,
        in_specs=[pl.BlockSpec(memory_space=pl.ANY)] * 6,
        out_specs=[pl.BlockSpec(memory_space=pl.ANY)] * 6,
        scratch_shapes=[pltpu.SemaphoreType.DMA((sems,)), pltpu.SemaphoreType.DMA((sems,))],
        compiler_params=pltpu.CompilerParams(collective_id=0, has_side_effects=True),
        name="gather",
    )(x, cot, wqkv, wproj, wup, wdown)


def scatter(line, plane, out_part, back_part, gq, gp, gu, gd):
    cores, rows, features = out_part.shape
    own = gq.shape[3]
    per_head, per_up = gq.shape[-1], gu.shape[-1]
    group = plane // 2
    p_rows, d_rows = gp.shape[0] // group, gd.shape[0] // group
    outs = (
        shape((rows, features), F32),
        shape((rows, features), F32),
        shape((own, 3 * cores * per_head), F32),
        shape((p_rows, features), F32),
        shape((own, cores * per_up), F32),
        shape((d_rows, features), F32),
    )
    sems = 16 * line + 16 * plane + 64
    vmem = pl.BlockSpec(memory_space=pltpu.VMEM)
    return pl.pallas_call(
        functools.partial(scatter_kernel, line, plane),
        out_shape=outs,
        in_specs=[vmem] * 6,
        out_specs=[vmem] * 6,
        scratch_shapes=[
            pltpu.VMEM((2, line, rows, features), BF16),
            pltpu.VMEM((2, line, rows, features), BF16),
            pltpu.VMEM((2, line, rows, features), BF16),
            pltpu.VMEM((plane, 3, line, own, per_head), BF16),
            pltpu.VMEM((plane, line, own, per_up), BF16),
            pltpu.VMEM((line, 3, own, per_head), BF16),
            pltpu.VMEM((line, own, per_up), BF16),
            pltpu.VMEM((cores, 3, own, per_head), BF16),
            pltpu.VMEM((cores, own, per_up), BF16),
            pltpu.VMEM((plane, p_rows // 2, features), BF16),
            pltpu.VMEM((plane, d_rows // 2, features), BF16),
            pltpu.SemaphoreType.DMA((sems,)),
            pltpu.SemaphoreType.DMA((sems,)),
        ],
        compiler_params=pltpu.CompilerParams(
            collective_id=1, has_side_effects=True, vmem_limit_bytes=60 * 1024 * 1024
        ),
        name="scatter",
    )(out_part, back_part, gq, gp, gu, gd)


def dot(left, right):
    return jnp.dot(left, right, preferred_element_type=F32)


def local(
    inputs,
    cotangent,
    attn_gain,
    attn_shift,
    qkv_weight,
    qkv_bias,
    proj_weight,
    proj_bias,
    mlp_gain,
    mlp_shift,
    up_weight,
    up_bias,
    down_weight,
    down_bias,
):
    owners = lax.axis_size("fsdp")
    replicas = lax.axis_size("replica")
    rows, features = inputs.shape
    line, plane = degrees(owners, features)
    cores = 2 * line
    count = cores * rows
    seqs = count // SEQ
    head_dim = features // H
    t = lax.axis_index("fsdp") // plane
    core = lax.rem(lax.axis_index("replica"), 2)
    piece = 2 * t + core

    vectors = (attn_gain, attn_shift, qkv_bias, proj_bias, mlp_gain, mlp_shift, up_bias, down_bias)
    packed = lax.all_gather(jnp.concatenate(vectors), "fsdp", axis=0, tiled=False).astype(F32)
    full, start = [], 0
    for vector in vectors:
        full.append(packed[:, start : start + vector.shape[0]].reshape(-1))
        start += vector.shape[0]
    g_attn, b_attn, b_qkv, b_proj, g_mlp, b_mlp, b_up, b_down = full
    x_all, cot_all, wq, wp, wu, wd = gather(
        line, plane, inputs, cotangent, qkv_weight, proj_weight, up_weight, down_weight
    )
    width, hidden = features // cores, up_weight.shape[1] // cores
    heads = width // head_dim
    x_all = x_all.reshape(count, features)
    cot_all = cot_all.reshape(count, features)
    wu = wu.reshape(features, hidden)
    wq = [wq[part].reshape(features, width) for part in range(3)]

    residual = x_all.astype(F32)
    normed, unit, inverse = normalize(residual, g_attn, b_attn)
    attn_in = normed.astype(BF16)
    mlp_in = (unit * g_mlp + b_mlp).astype(BF16)
    projected = []
    for part in range(3):
        bias = lax.dynamic_slice_in_dim(b_qkv, part * features + piece * width, width)
        projected.append((dot(attn_in, wq[part]) + bias).reshape(seqs, SEQ, heads, head_dim))
    cosine, sine = rotary_tables()
    queries = rotate(projected[0], cosine, sine, False).astype(BF16)
    keys_rot = rotate(projected[1], cosine, sine, False).astype(BF16)
    values = projected[2].astype(BF16)
    scores = masked_scores(queries, keys_rot)
    peak = jnp.max(scores, axis=-1, keepdims=True)
    logsum = peak + jnp.log(jnp.sum(jnp.exp(scores - peak), axis=-1, keepdims=True))
    probs = jnp.exp(scores - logsum)
    weights = probs.astype(BF16)
    context = product("bhqk,bkhd->bqhd", weights, values).astype(BF16).reshape(count, width)
    pre = dot(mlp_in, wu) + lax.dynamic_slice_in_dim(b_up, piece * hidden, hidden)
    activated = jax.nn.gelu(pre, approximate=False).astype(BF16)
    out_part = (dot(context, wp) + dot(activated, wd)).astype(BF16)

    g_down = dot(activated.T, cot_all).astype(BF16)
    grad_pre = dot(cot_all, wd.T) * gelu_slope(pre)
    up_sum = jnp.sum(grad_pre, axis=0)
    grad_pre_b = grad_pre.astype(BF16)
    g_up = dot(mlp_in.T, grad_pre_b).astype(BF16)
    grad_mlp_in = dot(grad_pre_b, wu.T)
    g_proj = dot(context.T, cot_all).astype(BF16)
    grad_context = dot(cot_all, wp.T).astype(BF16).reshape(queries.shape)
    grad_probs = product("bqhd,bkhd->bhqk", grad_context, values)
    grad_values = product("bhqk,bqhd->bkhd", weights, grad_context)
    grad_scores = (
        probs
        * (grad_probs - jnp.sum(probs * grad_probs, axis=-1, keepdims=True))
        * head_dim ** (-0.5)
    ).astype(BF16)
    grad_queries = product("bhqk,bkhd->bqhd", grad_scores, keys_rot)
    grad_keys = product("bhqk,bqhd->bkhd", grad_scores, queries)
    grads = [
        rotate(grad_queries, cosine, sine, True).reshape(count, width),
        rotate(grad_keys, cosine, sine, True).reshape(count, width),
        grad_values.reshape(count, width),
    ]
    qkv_sums = [jnp.sum(g, axis=0) for g in grads]
    grads_b = [g.astype(BF16) for g in grads]
    g_qkv = jnp.stack([dot(attn_in.T, g).astype(BF16) for g in grads_b])
    grad_attn_in = sum(dot(g, w.T) for g, w in zip(grads_b, wq))
    back_part = (grad_attn_in * g_attn + grad_mlp_in * g_mlp).astype(BF16)
    attn_gain_sum = jnp.sum(grad_attn_in * unit, axis=0)
    attn_shift_sum = jnp.sum(grad_attn_in, axis=0)
    mlp_gain_sum = jnp.sum(grad_mlp_in * unit, axis=0)
    mlp_shift_sum = jnp.sum(grad_mlp_in, axis=0)

    own = features // owners
    out_sum, back_sum, gw_qkv, gw_proj, gw_up, gw_down = scatter(
        line,
        plane,
        out_part.reshape(cores, rows, features),
        back_part.reshape(cores, rows, features),
        g_qkv.reshape(3, line, plane, own, width),
        g_proj,
        g_up.reshape(line, plane, own, hidden),
        g_down,
    )
    mine = inputs.astype(F32)
    upstream = cotangent.astype(F32)
    output = (mine + out_sum + (b_proj + b_down)).astype(BF16)
    _, unit_own, inverse_own = normalize(mine, g_attn, b_attn)
    back = inverse_own * (
        back_sum
        - jnp.mean(back_sum, axis=-1, keepdims=True)
        - unit_own * jnp.mean(back_sum * unit_own, axis=-1, keepdims=True)
    )
    grad_inputs = (upstream + back).astype(BF16)

    up_full = lax.dynamic_update_slice_in_dim(
        jnp.zeros((cores * hidden,), F32), up_sum, piece * hidden, 0
    )
    qkv_full = jnp.zeros((3 * features,), F32)
    for part in range(3):
        qkv_full = lax.dynamic_update_slice_in_dim(
            qkv_full, qkv_sums[part], part * features + piece * width, 0
        )
    small = (
        attn_gain_sum,
        attn_shift_sum,
        qkv_full,
        jnp.sum(upstream, axis=0),
        mlp_gain_sum,
        mlp_shift_sum,
        up_full,
    )
    packed = jnp.concatenate([v.reshape(owners, -1) for v in small], axis=1)
    packed = lax.psum(packed, ("fsdp", "replica"))
    packed = lax.dynamic_slice_in_dim(packed, lax.axis_index("fsdp"), 1, 0)[0]
    rest, start = [], 0
    for vector in small:
        size = vector.shape[0] // owners
        rest.append(packed[start : start + size])
        start += size
    if replicas > 2:
        groups = [[j for j in range(replicas) if j % 2 == k] for k in range(2)]
        gw_qkv, gw_proj, gw_up, gw_down = lax.psum(
            (gw_qkv, gw_proj, gw_up, gw_down), "replica", axis_index_groups=groups
        )
    return (
        output,
        grad_inputs,
        rest[0],
        rest[1],
        gw_qkv,
        rest[2],
        gw_proj,
        rest[3],
        rest[4],
        rest[5],
        gw_up,
        rest[6],
        gw_down,
        rest[3],
    )


def solution(mesh):
    return jax.shard_map(
        local,
        mesh=mesh,
        in_specs=(
            P(("fsdp", "replica"), None),
            P(("fsdp", "replica"), None),
            P("fsdp"),
            P("fsdp"),
            P("fsdp", None),
            P("fsdp"),
            P("fsdp", None),
            P("fsdp"),
            P("fsdp"),
            P("fsdp"),
            P("fsdp", None),
            P("fsdp"),
            P("fsdp", None),
            P("fsdp"),
        ),
        out_specs=(
            P(("fsdp", "replica"), None),
            P(("fsdp", "replica"), None),
            P("fsdp"),
            P("fsdp"),
            P("fsdp", None),
            P("fsdp"),
            P("fsdp", None),
            P("fsdp"),
            P("fsdp"),
            P("fsdp"),
            P("fsdp", None),
            P("fsdp"),
            P("fsdp", None),
            P("fsdp"),
        ),
        check_vma=False,
    )
```

```python
import functools
import math

import jax
import jax.numpy as jnp
import numpy as np
from jax import lax
from jax.experimental import pallas as pl
from jax.experimental.pallas import tpu as pltpu
from jax.sharding import PartitionSpec as P

H = 16
ROT = 16
SEQ = 128


EPSILON = 1e-05
THETA = 10000.0
SQRT_HALF = 0.7071067811865476
INV_ROOT_TAU = 0.3989422804014327


MESH = pl.DeviceIdType.MESH
LANES = 128
BF16 = jnp.bfloat16
F32 = jnp.float32
VMEM_BYTES = 60 * 1024 * 1024


def degrees(owners, features):
    line = math.gcd(owners, features // (2 * LANES))
    return line, owners // line


class Place:
    def __init__(self, line, plane):
        self.line, self.plane = line, plane
        self.owner = lax.axis_index("fsdp")
        replica = lax.axis_index("replica")
        self.t = lax.div(self.owner, plane)
        self.i = lax.rem(self.owner, plane)
        self.c = lax.rem(replica, 2)
        self.base = replica - self.c

    def at(self, t, i, c):
        return (t * self.plane + i, self.base + c)

    def on_line(self, k):
        return lax.rem(self.t + (k + self.line), self.line)

    def in_plane(self, k):
        return lax.rem(self.i + (k + self.plane), self.plane)

    def ends(self, k):
        if self.line < 3 or k not in (1, self.line - 1):
            return None
        return self.t == (0 if k == self.line - 1 else self.line - 1)

    def comes_far(self, k):
        if self.line < 3 or k not in (1, self.line - 1):
            return None
        return self.t == (self.line - 1 if k == self.line - 1 else 0)

    def greet(self):
        barrier = pltpu.get_barrier_semaphore()
        peers = [self.at(self.on_line(k), self.i, self.c) for k in range(1, self.line)]
        peers += [self.at(self.t, self.in_plane(k), self.c) for k in range(1, self.plane)]
        peers += [self.at(self.t, self.in_plane(k), 1 - self.c) for k in range(self.plane)]
        for peer in peers:
            pl.semaphore_signal(barrier, inc=1, device_id=peer, device_id_type=MESH)
        pl.semaphore_wait(barrier, len(peers))


class Copies:
    def __init__(self, send, recv):
        self.send, self.recv = send, recv
        self.used = 0
        self.last = []

    def slots(self, count):
        first = self.used
        self.used += count
        return first

    def push(self, src, dst, peer, slot, land=None):
        pltpu.make_async_remote_copy(
            src_ref=src,
            dst_ref=dst,
            send_sem=self.send.at[slot],
            recv_sem=self.recv.at[slot if land is None else land],
            device_id=peer,
            device_id_type=MESH,
        ).start()

    def local(self, src, dst, slot):
        pltpu.make_async_copy(src, dst, self.recv.at[slot]).start()

    def arrived(self, ref, slot):
        pltpu.make_async_copy(ref, ref, self.recv.at[slot]).wait()

    def left(self, ref, slot):
        pltpu.make_async_copy(ref, ref, self.send.at[slot]).wait()

    def later(self, ref, slots, when=None):
        def done():
            for slot in slots:
                self.left(ref, slot)

        self.last.append(done if when is None else lambda: pl.when(when)(done))

    def finish(self):
        for done in self.last:
            done()


def block(index, size):
    return pl.ds(pl.multiple_of(index * size, size), size)


def dot(left, right):
    return jnp.dot(left, right, preferred_element_type=F32)


def dot_last(left, right):
    return lax.dot_general(left, right, (((1,), (1,)), ((), ())), preferred_element_type=F32)


def exact_dot(left, right):
    return jnp.dot(left, right, preferred_element_type=F32, precision=lax.Precision.HIGHEST)


def counter(dims, axis):
    return lax.broadcasted_iota(jnp.int32, dims, axis)


def holder(index, width, count):
    found = jnp.zeros_like(index)
    for k in range(1, count):
        found = found + (index >= k * width).astype(jnp.int32)
    return found


class Refs:
    def __init__(self, refs, named):
        self.x, self.cot, self.wqkv, self.wproj, self.wup, self.wdown = refs[:6]
        self.vectors = refs[6:14]
        self.cosine, self.back_sine, self.fore_sine = refs[14:17]
        self.send, self.recv = refs[-2:]
        self.__dict__.update(zip(named, refs[17:-2]))


def layer_kernel(line, plane, head_dim, named, *refs):
    r = Refs(refs, named)
    me = Place(line, plane)
    t, i, c = me.t, me.i, me.c
    net = Copies(r.send, r.recv)
    owners, cores, group = line * plane, 2 * line, plane // 2
    x, cot, wqkv, wup = r.x, r.cot, r.wqkv, r.wup
    x_all, cot_all, wq, wp, wu, wd = r.x_all, r.cot_all, r.wq, r.wp, r.wu, r.wd
    rows, features = x.shape
    count = cores * rows
    pair = 2 * rows
    width = features // cores
    hidden = wup.shape[1] // cores
    own = features // owners
    span = features // line
    heads = width // head_dim
    piece = 2 * t + c
    mine = block(piece, rows)
    partner = me.at(t, i, 1 - c)
    v = r.vectors
    vec_own, vec_all = r.vec_own, r.vec_all
    reach = vec_own.shape[1]

    relays, adders = [], []
    if line > 2:
        adders = [(line - 2, 1), (2 % line, line - 2)]
        relays = [(line - 2, line - 2, 1, line - 1), (2 % line, 1, -1, 1)]
    relay_first = sorted({at_k for at_k, *_ in relays})
    relay_last = [k for k in range(1, line) if k not in relay_first]

    me.greet()

    vec_own[...] = jnp.zeros_like(vec_own)
    for n in range(8):
        size = v[n].shape[0]
        vec_own[n : n + 1, :size] = v[n][...].astype(F32).reshape(1, size)
    vec_all[me.owner] = vec_own[...]
    vec_first = net.slots(plane)
    for k in range(1, plane):
        net.push(vec_own, vec_all.at[me.owner], me.at(t, me.in_plane(k), c), vec_first + k)
    net.later(vec_own, range(vec_first + 1, vec_first + plane))

    col_slot = net.slots(4 * line)
    shard = pl.ds(pl.multiple_of(t * span + i * own, own), own)
    def move(k, n, src, dst):
        slot = col_slot + 4 * k + n
        if k == 0:
            net.local(src, dst, slot)
        else:
            net.push(src, dst, me.at(me.on_line(k), i, c), slot)
            net.later(dst, [slot])

    for k in range(line):
        for part in range(3):
            at = (part * cores + 2 * me.on_line(k) + c) * width
            src = wqkv.at[:, pl.ds(pl.multiple_of(at, LANES), width)]
            move(k, part, src, wq.at[shard, part * width : (part + 1) * width])
    for k in range(line):
        move(k, 3, wup.at[:, block(2 * me.on_line(k) + c, hidden)], wu.at[shard])

    def send_tokens(src, whole):
        line_slot = net.slots(line)
        pair_slot = net.slots(line)
        pass_slot = net.slots(2)
        for k in relay_first + relay_last:
            far = me.ends(k)
            near = None if far is None else jnp.logical_not(far)
            send = lambda: net.push(
                src, whole.at[mine], me.at(me.on_line(k), i, c), line_slot + k
            )
            send() if near is None else pl.when(near)(send)
            net.later(whole.at[mine], [line_slot + k], near)
        net.local(src, whole.at[mine], line_slot)
        net.push(src, whole.at[mine], partner, pair_slot)
        net.later(whole.at[mine], range(pair_slot, pair_slot + line))
        return line_slot, pair_slot, pass_slot

    def pass_tokens(whole, slots, distances):
        line_slot, pair_slot, pass_slot = slots
        for k in distances:
            ref = whole.at[block(2 * me.on_line(-k) + c, rows)]
            net.arrived(ref, line_slot + k)
            for n, (at_k, at_t, step, land) in enumerate(relays):
                if k == at_k:

                    @pl.when(t == at_t)
                    def _():
                        peer = me.at(me.on_line(step), i, c)
                        net.push(ref, ref, peer, pass_slot + n, line_slot + land)

                    net.later(ref, [pass_slot + n], t == at_t)
            net.push(ref, ref, partner, pair_slot + k)

    def other_tokens(whole, slots):
        for k in range(line):
            net.arrived(whole.at[block(2 * me.on_line(-k) + 1 - c, rows)], slots[1] + k)
        net.arrived(whole.at[mine], slots[0])

    x_slots = send_tokens(x, x_all)

    def rows_out(source, whole):
        height = source.shape[0]
        half = height // 2
        core = lax.div(i, group)
        src = source.at[block(c, half)]
        dst = whole.at[
            pl.ds(pl.multiple_of(lax.rem(i, group) * height + c * half, half), half)
        ]
        first = net.slots(2 * plane)
        away = net.slots(plane)
        for k in range(1, plane):
            net.push(src, dst, me.at(t, me.in_plane(k), core), away + k, first + 2 * k + c)
        net.later(dst, range(away + 1, away + plane))

        @pl.when(core == c)
        def _():
            net.local(src, dst, first + c)

        @pl.when(core != c)
        def _():
            net.push(src, dst, me.at(t, i, core), away, first + c)

        net.last.append(lambda: pl.when(core != c)(lambda: net.left(dst, away)))

        def wait():
            for k in range(plane):
                origin = me.in_plane(-k)

                @pl.when(lax.div(origin, group) == c)
                def _():
                    for s in range(2):
                        at = lax.rem(origin, group) * height + s * half
                        net.arrived(
                            whole.at[pl.ds(pl.multiple_of(at, half), half)], first + 2 * k + s
                        )

        return wait

    wp_wait = rows_out(r.wproj, wp)
    wd_wait = rows_out(r.wdown, wd)

    onward = net.slots(2)

    def strip(source, owner):
        return pl.ds(pl.multiple_of(source * span + owner * own, own), own)

    for k in range(1, plane):
        origin = me.in_plane(-k)
        net.arrived(vec_all.at[t * plane + origin], vec_first + k)
    vec_second = net.slots(line)
    bundle = vec_all.at[pl.ds(t * plane, plane)]
    for k in range(1, line):
        net.push(bundle, bundle, me.at(me.on_line(k), i, c), vec_second + k)
    net.later(bundle, range(vec_second + 1, vec_second + line))

    def columns_on(whole, n):
        for k in range(line):
            at = strip(me.on_line(-k), i)
            if n == 0:
                for part in range(3):
                    lanes = slice(part * width, (part + 1) * width)
                    net.arrived(whole.at[at, lanes], col_slot + 4 * k + part)
            else:
                net.arrived(whole.at[at], col_slot + 4 * k + 3)
            for j in range(1, plane):
                net.push(whole.at[at], whole.at[at], me.at(t, me.in_plane(j), c), onward + n)
        net.later(whole.at[: line * (plane - 1) * own], [onward + n])

    columns_on(wq, 0)
    columns_on(wu, 1)

    def wait_columns(whole, n):
        net.arrived(whole.at[: line * (plane - 1) * own], onward + n)

    pass_tokens(x_all, x_slots, relay_first + relay_last)
    cot_slots = send_tokens(cot, cot_all)

    for k in range(1, line):
        at = vec_all.at[pl.ds(me.on_line(-k) * plane, plane)]
        net.arrived(at, vec_second + k)
    flat = vec_all[...].reshape(owners * 8, reach).astype(BF16)

    def unpack(index, size):
        keeper = holder(index, size, owners)
        spread = (counter((size, index.shape[1]), 0) == index - keeper * size).astype(BF16)
        return dot(flat[:, :size], spread), keeper

    index = counter((1, features), 1)
    spread, keeper = unpack(index, own)
    spread = spread.reshape(owners, 8, features)
    keep = counter((owners, 8, features), 0) == keeper.reshape(1, 1, features)
    r.rows8[...] = jnp.sum(jnp.where(keep, spread, 0.0), axis=0)

    index = counter((1, 3 * width), 1)
    part = holder(index, width, 3)
    index = index + part * (features - width) + piece * width
    spread, keeper = unpack(index, 3 * own)
    keep = counter((owners * 8, 3 * width), 0) == keeper * 8 + 6
    r.bias_q[...] = jnp.sum(jnp.where(keep, spread, 0.0), axis=0, keepdims=True)
    index = counter((1, hidden), 1) + piece * hidden
    spread, keeper = unpack(index, v[7].shape[0])
    keep = counter((owners * 8, hidden), 0) == keeper * 8 + 7
    r.bias_u[...] = jnp.sum(jnp.where(keep, spread, 0.0), axis=0, keepdims=True)
    g_attn, b_attn, g_mlp, b_mlp = (r.rows8[n : n + 1, :] for n in range(4))

    attn_in, mlp_in = r.attn_in, r.mlp_in
    other_tokens(x_all, x_slots)

    def norm_step(j, carry):
        at = block(j, rows)
        data = x_all[at].astype(F32)
        mean = jnp.mean(data, axis=-1, keepdims=True)
        centered = data - mean
        inverse = lax.rsqrt(jnp.mean(centered * centered, axis=-1, keepdims=True) + EPSILON)
        r.mean[at] = mean
        r.inverse[at] = inverse
        unit = centered * inverse
        a = (unit * g_attn + b_attn).astype(BF16)
        m = (unit * g_mlp + b_mlp).astype(BF16)
        attn_in[at] = a
        mlp_in[at] = m
        r.attn_in_t[:, at] = a.T
        r.mlp_in_t[:, at] = m.T
        return carry

    lax.fori_loop(0, cores, norm_step, 0)

    half_rot = ROT // 2

    def turn(data, sign):
        seqs = data.shape[0] // SEQ
        cosine, back_sine, fore_sine = (
            jnp.concatenate([table[...]] * seqs, axis=0) if seqs > 1 else table[...]
            for table in (r.cosine, r.back_sine, r.fore_sine)
        )
        moved = (
            pltpu.roll(data, data.shape[1] - half_rot, 1) * back_sine
            + pltpu.roll(data, half_rot, 1) * fore_sine
        )
        return data * cosine + (moved if sign > 0 else -moved)

    wait_columns(wq, 0)

    def project_step(j, carry):
        at = block(j, pair)
        projected = dot(attn_in[at], wq[...]) + r.bias_q[...]
        r.q_s[at] = turn(projected[:, :width], 1).astype(BF16)
        r.k_s[at] = turn(projected[:, width : 2 * width], 1).astype(BF16)
        r.v_s[at] = projected[:, 2 * width :].astype(BF16)
        return carry

    lax.fori_loop(0, line, project_step, 0)

    lane = counter((SEQ, width), 1)

    def of_head(data, h):
        inside = (lane >= h * head_dim) & (lane < (h + 1) * head_dim)
        return jnp.where(inside, data, jnp.zeros_like(data))

    scale = head_dim ** (-0.5)

    def attend_step(s, carry):
        at = block(s, SEQ)
        queries, keys_rot, values = r.q_s[at], r.k_s[at], r.v_s[at]
        causal = counter((SEQ, SEQ), 0) >= counter((SEQ, SEQ), 1)
        total = jnp.zeros((SEQ, width), F32)
        for h in range(heads):
            scores = dot_last(of_head(queries, h), keys_rot) * scale
            scores = jnp.where(causal, scores, -jnp.inf)
            peak = jnp.max(scores, axis=-1, keepdims=True)
            logsum = peak + jnp.log(jnp.sum(jnp.exp(scores - peak), axis=-1, keepdims=True))
            probs = jnp.exp(scores - logsum)
            r.probs[s, h] = probs
            total = total + dot(probs.astype(BF16), of_head(values, h))
        context = total.astype(BF16)
        r.ctx[at] = context
        r.ctx_t[:, at] = context.T
        return carry

    lax.fori_loop(0, count // SEQ, attend_step, 0)

    pass_tokens(cot_all, cot_slots, relay_first)
    wait_columns(wu, 1)

    def hidden_step(j, carry):
        at = block(j, pair)
        pre = dot(mlp_in[at], wu[...]) + r.bias_u[...]
        chance = 0.5 * (1.0 + lax.erf(pre * SQRT_HALF))
        act = (pre * chance).astype(BF16)
        r.slope[at] = chance + pre * jnp.exp(-0.5 * pre * pre) * INV_ROOT_TAU
        r.act[at] = act
        r.act_t[:, at] = act.T
        return carry

    lax.fori_loop(0, line, hidden_step, 0)
    wp_wait()
    wd_wait()

    rows_in, rows_mid, rows_end = r.rows_in, r.rows_mid, r.rows_end
    swap_slot = net.slots(2 * line)
    end_slot = net.slots(2 * line)

    def swap(n, part, j):
        net.push(
            part.at[block(2 * j + 1 - c, rows)], rows_in.at[n, j], partner, swap_slot + n * line + j
        )

    relay_slot = net.slots(4)
    relay_in = r.relay_in

    def send_sum(n, k):
        slot = end_slot + n * line + k
        to = me.on_line(k)
        net.push(rows_mid.at[n, to], rows_end.at[n, k], me.at(to, i, c), slot)

    def add_up(n, part):
        for k in [line - 1] + list(range(1, line - 1)) + [line] if line > 1 else [line]:
            to = me.on_line(k)
            net.arrived(rows_in.at[n, to], swap_slot + n * line + to)
            both = part[block(2 * to + c, rows)].astype(F32) + rows_in[n, to].astype(F32)
            rows_mid[n, to] = both.astype(BF16)
            if k == line:
                continue
            direct = jnp.bool_(True)
            far = me.ends(k)
            if far is not None:
                way = 0 if k == line - 1 else 1

                @pl.when(far)
                def _():
                    peer = me.at(line - 2 if k == 1 else 1, i, c)
                    slot = relay_slot + 2 * n + way
                    net.push(rows_mid.at[n, to], relay_in.at[n, way], peer, slot)

                net.later(rows_mid.at[n, to], [relay_slot + 2 * n + way], far)
                direct = jnp.logical_not(far)
            net.later(rows_mid.at[n, to], [end_slot + n * line + k], direct)
            for at_k, at_t in adders:
                if k == at_k:
                    direct = jnp.logical_and(direct, t != at_t)
            pl.when(direct)(lambda: send_sum(n, k))
        net.later(rows_in.at[n, 0], range(swap_slot + n * line, swap_slot + (n + 1) * line))

    def relay_up(n):
        for way, (k, at_t) in enumerate(adders):

            @pl.when(t == at_t)
            def _():
                to = me.on_line(k)
                net.arrived(relay_in.at[n, way], relay_slot + 2 * n + way)
                both = rows_mid[n, to].astype(F32) + relay_in[n, way].astype(F32)
                rows_mid[n, to] = both.astype(BF16)
                send_sum(n, k)

    def row_total(n):
        total = r.total
        total[...] = rows_mid[n, t].astype(F32)
        for k in range(1, line):

            def more():
                net.arrived(rows_end.at[n, k], end_slot + n * line + k)
                total[...] += rows_end[n, k].astype(F32)

            far = me.comes_far(k)
            more() if far is None else pl.when(jnp.logical_not(far))(more)
        return total[...]

    def out_step(j, carry):
        at = block(j, pair)
        part = dot(r.ctx[at], wp[...]) + dot(r.act[at], wd[...])
        r.out_part[at] = part.astype(BF16)
        swap(0, r.out_part, j)
        return carry

    lax.fori_loop(0, line, out_step, 0)
    add_up(0, r.out_part)

    pass_tokens(cot_all, cot_slots, relay_last)
    other_tokens(cot_all, cot_slots)

    def rows_back(source, landing):
        height = source.shape[0] // group
        half = height // 2
        slot = net.slots(2 * plane)
        for k in range(plane):
            to = me.in_plane(k)

            @pl.when(lax.div(to, group) == c)
            def _():
                for s in range(2):
                    src = source.at[
                        pl.ds(pl.multiple_of(lax.rem(to, group) * height + s * half, half), half)
                    ]
                    send = lambda: net.push(
                        src, landing.at[k], me.at(t, to, s), slot + 2 * k + s, slot + k
                    )
                    if k == 0:
                        pl.when(c == s)(lambda: net.local(src, landing.at[k], slot + k))
                        pl.when(c != s)(send)
                    else:
                        send()

        def arrive():
            for k in range(plane):
                net.arrived(landing.at[k], slot + k)

        def leave():
            for k in range(plane):
                to = me.in_plane(k)

                @pl.when(lax.div(to, group) == c)
                def _():
                    for s in range(2):
                        done = lambda: net.left(landing.at[k], slot + 2 * k + s)
                        if k == 0:
                            pl.when(c != s)(done)
                        else:
                            done()

        net.last.append(leave)
        return arrive

    def down_step(j, carry):
        at = block(j, LANES)
        r.gd[at] = dot(r.act_t[at], cot_all[...]).astype(BF16)
        return carry

    lax.fori_loop(0, hidden // LANES, down_step, 0)
    relay_up(0)
    d_arrive = rows_back(r.gd, r.d_in)

    sums = r.sums
    sums[...] = jnp.zeros_like(sums)

    def slope_step(j, carry):
        at = block(j, pair)
        grad = dot_last(cot_all[at], wd[...]) * r.slope[at]
        sums[5:6, :hidden] += jnp.sum(grad, axis=0, keepdims=True)
        r.gpre[at] = grad.astype(BF16)
        r.gctx[at] = dot_last(cot_all[at], wp[...]).astype(BF16)
        return carry

    lax.fori_loop(0, line, slope_step, 0)

    q_in, u_in = r.q_in, r.u_in
    col_back = net.slots(2 * plane)

    def up_step(j, carry):
        grad = dot(r.mlp_in_t[block(j, span)], r.gpre[...]).astype(BF16)
        r.gu[j] = grad.reshape(plane, own, hidden)
        return carry

    lax.fori_loop(0, line, up_step, 0)
    for k in range(1, plane):
        to = me.in_plane(k)
        net.push(r.gu.at[:, to], u_in.at[k], me.at(t, to, c), col_back + 2 * k + 1)
        net.later(u_in.at[k], [col_back + 2 * k + 1])

    def attend_back_step(s, carry):
        at = block(s, SEQ)
        queries, keys_rot, values, upper = r.q_s[at], r.k_s[at], r.v_s[at], r.gctx[at]
        g_queries = jnp.zeros((SEQ, width), F32)
        g_keys = jnp.zeros((SEQ, width), F32)
        g_values = jnp.zeros((SEQ, width), F32)
        for h in range(heads):
            probs = r.probs[s, h]
            upper_h = of_head(upper, h)
            g_probs = dot_last(upper_h, values)
            g_values = g_values + dot(probs.astype(BF16).T, upper_h)
            g_scores = (
                probs * (g_probs - jnp.sum(probs * g_probs, axis=-1, keepdims=True)) * scale
            ).astype(BF16)
            g_queries = g_queries + dot(g_scores, of_head(keys_rot, h))
            g_keys = g_keys + dot(g_scores.T, of_head(queries, h))
        parts = (turn(g_queries, -1), turn(g_keys, -1), g_values)
        for n, grad in enumerate(parts):
            lanes = slice(n * width, (n + 1) * width)
            sums[6:7, lanes] += jnp.sum(grad, axis=0, keepdims=True)
            r.gcol[at, lanes] = grad.astype(BF16)
        return carry

    lax.fori_loop(0, count // SEQ, attend_back_step, 0)

    def back_step(j, carry):
        at = block(j, pair)
        unit = (x_all[at].astype(F32) - r.mean[at]) * r.inverse[at]
        g_a = dot_last(r.gcol[at], wq[...])
        sums[0:1, :] += jnp.sum(g_a * unit, axis=0, keepdims=True)
        sums[1:2, :] += jnp.sum(g_a, axis=0, keepdims=True)
        g_m = dot_last(r.gpre[at], wu[...])
        sums[2:3, :] += jnp.sum(g_m * unit, axis=0, keepdims=True)
        sums[3:4, :] += jnp.sum(g_m, axis=0, keepdims=True)
        part = g_a * r.rows8[0:1, :] + g_m * r.rows8[2:3, :]
        r.back_part[at] = part.astype(BF16)
        swap(1, r.back_part, j)
        return carry

    lax.fori_loop(0, line, back_step, 0)
    add_up(1, r.back_part)
    relay_up(1)
    sums[4:5, :] = jnp.sum(cot_all[mine].astype(F32), axis=0, keepdims=True)

    def qkv_step(j, carry):
        grad = dot(r.attn_in_t[block(j, span)], r.gcol[...]).astype(BF16)
        r.gq[j] = grad.reshape(plane, own, 3 * width)
        return carry

    lax.fori_loop(0, line, qkv_step, 0)
    for k in range(1, plane):
        to = me.in_plane(k)
        net.push(r.gq.at[:, to], q_in.at[k], me.at(t, to, c), col_back + 2 * k)
        net.later(q_in.at[k], [col_back + 2 * k])
    r.gp[...] = dot(r.ctx_t[...], cot_all[...]).astype(BF16)
    p_arrive = rows_back(r.gp, r.p_in)

    sums_in, sums_all = r.sums_in, r.sums_all
    sum_slot = net.slots(plane)
    for k in range(1, plane):
        net.push(sums, sums_in.at[k], me.at(t, me.in_plane(k), c), sum_slot + k)
    net.later(sums, range(sum_slot + 1, sum_slot + plane))

    q_mid, u_mid, q_end, u_end = r.q_mid, r.u_mid, r.q_end, r.u_end
    third = net.slots(2 * line)
    fourth = net.slots(2 * line)

    def column_total(n, source, landing, middle, end):
        for k in range(1, plane):
            net.arrived(landing.at[k], col_back + 2 * k + n)
        for b in range(line):
            total = source[b, i].astype(F32)
            for k in range(1, plane):
                total = total + landing[k, b].astype(F32)
            middle[b] = total.astype(BF16)
        for k in range(1, line):
            to = me.on_line(k)
            net.push(middle.at[to], end.at[piece], me.at(to, i, c), third + 2 * k + n)
            net.later(middle.at[to], [third + 2 * k + n])
        end[piece] = middle[t]
        net.push(end.at[piece], end.at[piece], partner, fourth + n)
        net.later(end.at[piece], [fourth + 2 * k + n for k in range(line)])

    def column_pass(n, end):
        for k in range(1, line):
            ref = end.at[2 * me.on_line(-k) + c]
            net.arrived(ref, third + 2 * k + n)
            net.push(ref, ref, partner, fourth + 2 * k + n)

    def column_end(n, end):
        for k in range(line):
            net.arrived(end.at[2 * me.on_line(-k) + 1 - c], fourth + 2 * k + n)

    column_total(1, r.gu, u_in, u_mid, u_end)

    half_slot = net.slots(2)

    def row_end(n, landing, whole, arrive):
        arrive()
        half = landing.shape[1]
        total = landing[0].astype(F32)
        for k in range(1, plane):
            total = total + landing[k].astype(F32)
        at = whole.at[block(c, half)]
        at[...] = total
        net.push(at, at, partner, half_slot + n)
        net.later(at, [half_slot + n])

    row_end(0, r.d_in, r.gd_out, d_arrive)

    for k in range(1, plane):
        net.arrived(sums_in.at[k], sum_slot + k)
    total = sums[...]
    for k in range(1, plane):
        total = total + sums_in[k]
    sums_all[piece] = total
    sum_second = net.slots(line)
    sum_third = net.slots(line)
    ref = sums_all.at[piece]
    for k in range(1, line):
        net.push(ref, ref, me.at(me.on_line(k), i, c), sum_second + k)
    net.push(ref, ref, partner, sum_third)
    net.later(ref, range(sum_second + 1, sum_second + line))
    net.later(ref, range(sum_third, sum_third + line))

    column_total(0, r.gq, q_in, q_mid, q_end)
    row_end(1, r.p_in, r.gp_out, p_arrive)

    for k in range(1, line):
        ref = sums_all.at[2 * me.on_line(-k) + c]
        net.arrived(ref, sum_second + k)
        net.push(ref, ref, partner, sum_third + k)
    column_pass(1, u_end)

    data = x_all[mine].astype(F32)
    bias = r.rows8[4:5, :] + r.rows8[5:6, :]
    r.output[...] = (data + row_total(0) + bias).astype(BF16)
    unit = (data - r.mean[mine]) * r.inverse[mine]
    grad = row_total(1)
    grad = r.inverse[mine] * (
        grad
        - jnp.mean(grad, axis=-1, keepdims=True)
        - unit * jnp.mean(grad * unit, axis=-1, keepdims=True)
    )
    r.grad_x[...] = (cot_all[mine].astype(F32) + grad).astype(BF16)

    column_pass(0, q_end)
    column_end(1, u_end)

    for k in range(line):
        net.arrived(sums_all.at[2 * me.on_line(-k) + 1 - c], sum_third + k)
    every = sums_all[...]
    total = every[0]
    for b in range(1, cores):
        total = total + every[b]
    chosen = counter((features, own), 0) == me.owner * own + counter((features, own), 1)
    r.five_out[...] = exact_dot(total, chosen.astype(F32))
    stacked = every.reshape(cores * 8, features)

    def pick(columns, size, keeper, column, row, out):
        chosen = (counter((columns, size), 0) == column).astype(F32)
        found = exact_dot(stacked[:, :columns], chosen)
        keep = counter((cores * 8, size), 0) == keeper * 8 + row
        out[...] = jnp.sum(jnp.where(keep, found, 0.0), axis=0, keepdims=True)

    size = v[7].shape[0]
    index = me.owner * size + counter((1, size), 1)
    keeper = holder(index, hidden, cores)
    pick(hidden, size, keeper, index - keeper * hidden, 5, r.bu_out)
    size = 3 * own
    index = me.owner * size + counter((1, size), 1)
    part = holder(index, features, 3)
    index = index - part * features
    keeper = holder(index, width, cores)
    pick(3 * width, size, keeper, index - keeper * width + part * width, 6, r.bq_out)

    column_end(0, q_end)
    for n, whole in enumerate((r.gd_out, r.gp_out)):
        half = whole.shape[0] // 2
        net.arrived(whole.at[block(1 - c, half)], half_slot + n)
    assert net.used <= r.send.shape[0]
    net.finish()


def finish_kernel(output, grad_x, q_end, u_end, gp, gd, five, bq, bu, *finals):
    (
        output_f,
        grad_x_f,
        gain_a,
        shift_a,
        gq_f,
        bq_f,
        gp_f,
        bp_f,
        gain_m,
        shift_m,
        gu_f,
        bu_f,
        gd_f,
        bd_f,
    ) = finals
    output_f[...] = output[...]
    grad_x_f[...] = grad_x[...]
    cores, _, hidden = u_end.shape
    width = q_end.shape[2] // 3
    for b in range(cores):
        gu_f[:, b * hidden : (b + 1) * hidden] = u_end[b].astype(F32)
        for part in range(3):
            at = (part * cores + b) * width
            gq_f[:, at : at + width] = q_end[b, :, part * width : (part + 1) * width].astype(F32)
    gp_f[...] = gp[...]
    gd_f[...] = gd[...]
    for n, leaf in enumerate((gain_a, shift_a, gain_m, shift_m, bp_f)):
        leaf[...] = five[n]
    bd_f[...] = five[4]
    bq_f[...] = bq[0]
    bu_f[...] = bu[0]


def turn_tables(width, head_dim):
    half = ROT // 2
    frequency = THETA ** (-2.0 * np.arange(half) / ROT)
    angles = np.arange(SEQ)[:, None] * frequency[None, :]
    cosine, sine = np.cos(angles), np.sin(angles)
    rest = head_dim - ROT
    heads = width // head_dim
    one = np.ones((SEQ, rest))
    none = np.zeros((SEQ, rest))
    zero = np.zeros((SEQ, half))
    tables = (
        [cosine, cosine, one],
        [-sine, zero, none],
        [zero, sine, none],
    )
    return [np.concatenate(parts * heads, axis=1).astype(np.float32) for parts in tables]


def local(
    inputs,
    cotangent,
    attn_gain,
    attn_shift,
    qkv_weight,
    qkv_bias,
    proj_weight,
    proj_bias,
    mlp_gain,
    mlp_shift,
    up_weight,
    up_bias,
    down_weight,
    down_bias,
):
    owners = lax.axis_size("fsdp")
    replicas = lax.axis_size("replica")
    rows, features = inputs.shape
    line, plane = degrees(owners, features)
    cores = 2 * line
    count = cores * rows
    head_dim = features // H
    width, hidden = features // cores, up_weight.shape[1] // cores
    own = features // owners
    proj_rows, down_rows = proj_weight.shape[0], down_weight.shape[0]
    heads = width // head_dim
    reach = -(-max(v.shape[0] for v in (attn_gain, qkv_bias, up_bias)) // LANES) * LANES

    vectors = (attn_gain, attn_shift, mlp_gain, mlp_shift, proj_bias, down_bias, qkv_bias, up_bias)
    outs = dict(
        output=((rows, features), BF16),
        grad_x=((rows, features), BF16),
        q_end=((cores, own, 3 * width), BF16),
        u_end=((cores, own, hidden), BF16),
        gp_out=((proj_rows, features), F32),
        gd_out=((down_rows, features), F32),
        five_out=((8, own), F32),
        bq_out=((1, 3 * own), F32),
        bu_out=((1, up_bias.shape[0]), F32),
    )
    scratch = dict(
        x_all=((count, features), BF16),
        cot_all=((count, features), BF16),
        wq=((features, 3 * width), BF16),
        wp=((width, features), BF16),
        wu=((features, hidden), BF16),
        wd=((hidden, features), BF16),
        vec_own=((8, reach), F32),
        vec_all=((owners, 8, reach), F32),
        rows8=((8, features), F32),
        bias_q=((1, 3 * width), F32),
        bias_u=((1, hidden), F32),
        mean=((count, 1), F32),
        inverse=((count, 1), F32),
        attn_in=((count, features), BF16),
        attn_in_t=((features, count), BF16),
        mlp_in=((count, features), BF16),
        mlp_in_t=((features, count), BF16),
        q_s=((count, width), BF16),
        k_s=((count, width), BF16),
        v_s=((count, width), BF16),
        probs=((count // SEQ, heads, SEQ, SEQ), F32),
        ctx=((count, width), BF16),
        ctx_t=((width, count), BF16),
        act=((count, hidden), BF16),
        act_t=((hidden, count), BF16),
        slope=((count, hidden), F32),
        gpre=((count, hidden), BF16),
        gcol=((count, 3 * width), BF16),
        gctx=((count, width), BF16),
        out_part=((count, features), BF16),
        back_part=((count, features), BF16),
        gq=((line, plane, own, 3 * width), BF16),
        gp=((width, features), BF16),
        gu=((line, plane, own, hidden), BF16),
        gd=((hidden, features), BF16),
        rows_in=((2, line, rows, features), BF16),
        rows_mid=((2, line, rows, features), BF16),
        rows_end=((2, line, rows, features), BF16),
        relay_in=((2, 2, rows, features), BF16),
        total=((rows, features), F32),
        q_in=((plane, line, own, 3 * width), BF16),
        u_in=((plane, line, own, hidden), BF16),
        q_mid=((line, own, 3 * width), BF16),
        u_mid=((line, own, hidden), BF16),
        p_in=((plane, proj_rows // 2, features), BF16),
        d_in=((plane, down_rows // 2, features), BF16),
        sums=((8, features), F32),
        sums_in=((plane, 8, features), F32),
        sums_all=((cores, 8, features), F32),
    )
    sems = 20 * line + 16 * plane
    vmem = pl.BlockSpec(memory_space=pltpu.VMEM)
    results = pl.pallas_call(
        functools.partial(layer_kernel, line, plane, head_dim, list(outs) + list(scratch)),
        out_shape=[jax.ShapeDtypeStruct(*outs[name]) for name in outs],
        in_specs=[pl.BlockSpec(memory_space=pl.ANY)] * 6 + [vmem] * 11,
        out_specs=[vmem] * len(outs),
        scratch_shapes=[pltpu.VMEM(*scratch[name]) for name in scratch]
        + [pltpu.SemaphoreType.DMA((sems,)), pltpu.SemaphoreType.DMA((sems,))],
        compiler_params=pltpu.CompilerParams(
            collective_id=0, has_side_effects=True, vmem_limit_bytes=VMEM_BYTES
        ),
        name="layer",
    )(
        inputs,
        cotangent,
        qkv_weight,
        proj_weight,
        up_weight,
        down_weight,
        *vectors,
        *turn_tables(width, head_dim),
    )
    gradients = (
        ((own,), F32),
        ((own,), F32),
        ((own, 3 * features), F32),
        ((3 * own,), F32),
        ((proj_rows, features), F32),
        ((own,), F32),
        ((own,), F32),
        ((own,), F32),
        ((own, cores * hidden), F32),
        (up_bias.shape, F32),
        ((down_rows, features), F32),
        ((own,), F32),
    )
    final = tuple(outs.values())[:2] + gradients
    final = pl.pallas_call(
        finish_kernel,
        out_shape=[jax.ShapeDtypeStruct(*leaf) for leaf in final],
        in_specs=[vmem] * len(outs),
        out_specs=[vmem] * len(final),
        compiler_params=pltpu.CompilerParams(vmem_limit_bytes=VMEM_BYTES),
        name="finish",
    )(*results)
    final = list(final)
    if replicas > 2:
        groups = [[j for j in range(replicas) if j % 2 == k] for k in range(2)]
        final[2:] = lax.psum(tuple(final[2:]), "replica", axis_index_groups=groups)
    return tuple(final)


def solution(mesh):
    return jax.shard_map(
        local,
        mesh=mesh,
        in_specs=(
            P(("fsdp", "replica"), None),
            P(("fsdp", "replica"), None),
            P("fsdp"),
            P("fsdp"),
            P("fsdp", None),
            P("fsdp"),
            P("fsdp", None),
            P("fsdp"),
            P("fsdp"),
            P("fsdp"),
            P("fsdp", None),
            P("fsdp"),
            P("fsdp", None),
            P("fsdp"),
        ),
        out_specs=(
            P(("fsdp", "replica"), None),
            P(("fsdp", "replica"), None),
            P("fsdp"),
            P("fsdp"),
            P("fsdp", None),
            P("fsdp"),
            P("fsdp", None),
            P("fsdp"),
            P("fsdp"),
            P("fsdp"),
            P("fsdp", None),
            P("fsdp"),
            P("fsdp", None),
            P("fsdp"),
        ),
        check_vma=False,
    )
```

```python
import functools
import math

import jax
import jax.numpy as jnp
import numpy as np
from jax import lax
from jax.experimental import pallas as pl
from jax.experimental.pallas import tpu as pltpu
from jax.sharding import PartitionSpec as P

H = 16
ROT = 16
SEQ = 128


EPSILON = 1e-05
THETA = 10000.0
SQRT_HALF = 0.7071067811865476
INV_ROOT_TAU = 0.3989422804014327


MESH = pl.DeviceIdType.MESH
LANES = 128
BF16 = jnp.bfloat16
F32 = jnp.float32
VMEM_BYTES = 48 * 1024 * 1024


def degrees(owners, features):
    line = math.gcd(owners, features // (2 * LANES))
    return line, owners // line


class Place:
    def __init__(self, line, plane):
        self.line, self.plane = line, plane
        self.owner = lax.axis_index("fsdp")
        replica = lax.axis_index("replica")
        self.t = lax.div(self.owner, plane)
        self.i = lax.rem(self.owner, plane)
        self.c = lax.rem(replica, 2)
        self.base = replica - self.c

    def at(self, t, i, c):
        return (t * self.plane + i, self.base + c)

    def on_line(self, k):
        return lax.rem(self.t + (k + self.line), self.line)

    def in_plane(self, k):
        return lax.rem(self.i + (k + self.plane), self.plane)

    def ends(self, k):
        if self.line < 3 or k not in (1, self.line - 1):
            return None
        return self.t == (0 if k == self.line - 1 else self.line - 1)

    def comes_far(self, k):
        if self.line < 3 or k not in (1, self.line - 1):
            return None
        return self.t == (self.line - 1 if k == self.line - 1 else 0)

    def greet(self):
        barrier = pltpu.get_barrier_semaphore()
        peers = [self.at(self.on_line(k), self.i, self.c) for k in range(1, self.line)]
        peers += [self.at(self.t, self.in_plane(k), self.c) for k in range(1, self.plane)]
        peers += [self.at(self.t, self.in_plane(k), 1 - self.c) for k in range(self.plane)]
        for peer in peers:
            pl.semaphore_signal(barrier, inc=1, device_id=peer, device_id_type=MESH)
        pl.semaphore_wait(barrier, len(peers))


class Copies:
    def __init__(self, send, recv):
        self.send, self.recv = send, recv
        self.used = 0
        self.last = []

    def slots(self, count):
        first = self.used
        self.used += count
        return first

    def push(self, src, dst, peer, slot, land=None):
        pltpu.make_async_remote_copy(
            src_ref=src,
            dst_ref=dst,
            send_sem=self.send.at[slot],
            recv_sem=self.recv.at[slot if land is None else land],
            device_id=peer,
            device_id_type=MESH,
        ).start()

    def local(self, src, dst, slot):
        pltpu.make_async_copy(src, dst, self.recv.at[slot]).start()

    def arrived(self, ref, slot):
        pltpu.make_async_copy(ref, ref, self.recv.at[slot]).wait()

    def left(self, ref, slot):
        pltpu.make_async_copy(ref, ref, self.send.at[slot]).wait()

    def later(self, ref, slots, when=None):
        def done():
            for slot in slots:
                self.left(ref, slot)

        self.last.append(done if when is None else lambda: pl.when(when)(done))

    def finish(self):
        for done in self.last:
            done()


def block(index, size):
    return pl.ds(pl.multiple_of(index * size, size), size)


def dot(left, right):
    return jnp.dot(left, right, preferred_element_type=F32)


def dot_last(left, right):
    return lax.dot_general(left, right, (((1,), (1,)), ((), ())), preferred_element_type=F32)


def exact_dot(left, right):
    return jnp.dot(left, right, preferred_element_type=F32, precision=lax.Precision.HIGHEST)


def counter(dims, axis):
    return lax.broadcasted_iota(jnp.int32, dims, axis)


def holder(index, width, count):
    found = jnp.zeros_like(index)
    for k in range(1, count):
        found = found + (index >= k * width).astype(jnp.int32)
    return found


class Refs:
    def __init__(self, refs, named):
        self.x, self.cot, self.wqkv, self.wproj, self.wup, self.wdown = refs[:6]
        self.small = refs[6:17]
        self.send, self.recv = refs[-2:]
        self.__dict__.update(zip(named, refs[17:-2]))


def layer_kernel(line, plane, head_dim, named, *refs):
    r = Refs(refs, named)
    me = Place(line, plane)
    t, i, c = me.t, me.i, me.c
    net = Copies(r.send, r.recv)
    owners, cores, group = line * plane, 2 * line, plane // 2
    x, cot, wqkv, wup = r.x, r.cot, r.wqkv, r.wup
    x_all, cot_all, wq, wp, wu, wd = r.x_all, r.cot_all, r.wq, r.wp, r.wu, r.wd
    rows, features = x.shape
    count = cores * rows
    pair = 2 * rows
    width = features // cores
    hidden = wup.shape[1] // cores
    own = features // owners
    span = features // line
    heads = width // head_dim
    piece = 2 * t + c
    mine = block(piece, rows)
    partner = me.at(t, i, 1 - c)
    small = [r.v0, r.v1, r.v2, r.v3, r.v4, r.v5, r.v6, r.v7, r.cosine, r.back_sine, r.fore_sine]
    v = small[:8]
    vec_own, vec_all = r.vec_own, r.vec_all
    reach = vec_own.shape[1]

    relays, adders = [], []
    if line > 2:
        adders = [(line - 2, 1), (2 % line, line - 2)]
        relays = [(line - 2, line - 2, 1, line - 1), (2 % line, 1, -1, 1)]
    relay_first = sorted({at_k for at_k, *_ in relays})
    relay_last = [k for k in range(1, line) if k not in relay_first]

    small_slot = net.slots(len(small))
    for n, ref in enumerate(small):
        net.local(r.small[n], ref, small_slot + n)
    me.greet()
    for n, ref in enumerate(small):
        net.arrived(ref, small_slot + n)

    vec_own[...] = jnp.zeros_like(vec_own)
    for n in range(8):
        size = v[n].shape[0]
        vec_own[n : n + 1, :size] = v[n][...].astype(F32).reshape(1, size)
    vec_all[me.owner] = vec_own[...]
    vec_first = net.slots(1)
    for k in range(1, plane):
        net.push(vec_own, vec_all.at[me.owner], me.at(t, me.in_plane(k), c), vec_first)
    net.later(vec_all.at[: plane - 1], [vec_first])

    col_slot = net.slots(2 * line)
    shard = pl.ds(pl.multiple_of(t * span + i * own, own), own)
    def move(k, n, src, dst):
        slot = col_slot + 2 * k + n
        if k == 0:
            net.local(src, dst, slot)
        else:
            net.push(src, dst, me.at(me.on_line(k), i, c), slot)

    for k in range(line):
        for part in range(3):
            at = (part * cores + 2 * me.on_line(k) + c) * width
            src = wqkv.at[:, pl.ds(pl.multiple_of(at, LANES), width)]
            move(k, 0, src, wq.at[shard, part * width : (part + 1) * width])
    for k in range(line):
        move(k, 1, wup.at[:, block(2 * me.on_line(k) + c, hidden)], wu.at[shard])

    def send_tokens(src, whole):
        line_slot = net.slots(line)
        pair_slot = net.slots(line)
        pass_slot = net.slots(2)
        for k in relay_first + relay_last:
            far = me.ends(k)
            near = None if far is None else jnp.logical_not(far)
            send = lambda: net.push(
                src, whole.at[mine], me.at(me.on_line(k), i, c), line_slot + k
            )
            net.later(whole.at[mine], [line_slot + k], near)
            for _, at_t, _, land in relays if line > 3 else []:
                if k == land:
                    ready = t != at_t
                    near = ready if near is None else jnp.logical_and(near, ready)
            send() if near is None else pl.when(near)(send)
        net.local(src, whole.at[mine], line_slot)
        net.push(src, whole.at[mine], partner, pair_slot)
        net.later(whole.at[mine], range(pair_slot, pair_slot + line))
        return line_slot, pair_slot, pass_slot, src

    def pass_tokens(whole, slots, distances):
        line_slot, pair_slot, pass_slot, src = slots
        for k in distances:
            ref = whole.at[block(2 * me.on_line(-k) + c, rows)]
            net.arrived(ref, line_slot + k)
            for n, (at_k, at_t, step, land) in enumerate(relays):
                if k == at_k:

                    @pl.when(t == at_t)
                    def _():
                        peer = me.at(me.on_line(step), i, c)
                        net.push(ref, ref, peer, pass_slot + n, line_slot + land)
                        if line > 3:
                            peer = me.at(me.on_line(-step), i, c)
                            net.push(src, whole.at[mine], peer, line_slot + land)

                    net.later(ref, [pass_slot + n], t == at_t)
            net.push(ref, ref, partner, pair_slot + k)

    def other_tokens(whole, slots):
        for k in range(line):
            net.arrived(whole.at[block(2 * me.on_line(-k) + 1 - c, rows)], slots[1] + k)
        net.arrived(whole.at[mine], slots[0])

    x_slots = send_tokens(x, x_all)

    def rows_out(source, whole):
        height = source.shape[0]
        half = height // 2
        core = lax.div(i, group)
        src = source.at[block(c, half)]
        dst = whole.at[
            pl.ds(pl.multiple_of(lax.rem(i, group) * height + c * half, half), half)
        ]
        first = net.slots(2 * plane)
        away = net.slots(plane)
        for k in range(1, plane):
            net.push(src, dst, me.at(t, me.in_plane(k), core), away + k, first + 2 * k + c)
        net.later(dst, range(away + 1, away + plane))

        @pl.when(core == c)
        def _():
            net.local(src, dst, first + c)

        @pl.when(core != c)
        def _():
            net.push(src, dst, me.at(t, i, core), away, first + c)

        net.last.append(lambda: pl.when(core != c)(lambda: net.left(dst, away)))

        def wait():
            for k in range(plane):
                origin = me.in_plane(-k)

                @pl.when(lax.div(origin, group) == c)
                def _():
                    for s in range(2):
                        at = lax.rem(origin, group) * height + s * half
                        net.arrived(
                            whole.at[pl.ds(pl.multiple_of(at, half), half)], first + 2 * k + s
                        )

        return wait

    wp_wait = rows_out(r.wproj, wp)
    wd_wait = rows_out(r.wdown, wd)

    onward = net.slots(2)

    def strip(source, owner):
        return pl.ds(pl.multiple_of(source * span + owner * own, own), own)

    net.arrived(vec_all.at[: plane - 1], vec_first)
    vec_second = net.slots(1)
    bundle = vec_all.at[pl.ds(t * plane, plane)]
    for k in range(1, line):
        net.push(bundle, bundle, me.at(me.on_line(k), i, c), vec_second)
    others = vec_all.at[: (line - 1) * plane]
    if line > 1:
        net.later(others, [vec_second])

    def columns_on(whole, n):
        for k in range(line):
            at = strip(me.on_line(-k), i)
            net.arrived(whole.at[at], col_slot + 2 * k + n)
            if k > 0:
                net.later(whole.at[at], [col_slot + 2 * k + n])
            for j in range(1, plane):
                net.push(whole.at[at], whole.at[at], me.at(t, me.in_plane(j), c), onward + n)
        net.later(whole.at[: line * (plane - 1) * own], [onward + n])

    columns_on(wq, 0)
    columns_on(wu, 1)

    def wait_columns(whole, n):
        net.arrived(whole.at[: line * (plane - 1) * own], onward + n)

    pass_tokens(x_all, x_slots, relay_first + relay_last)
    cot_slots = send_tokens(cot, cot_all)

    if line > 1:
        net.arrived(others, vec_second)
    flat = vec_all[...].reshape(owners * 8, reach).astype(BF16)

    def unpack(index, size):
        keeper = holder(index, size, owners)
        spread = (counter((size, index.shape[1]), 0) == index - keeper * size).astype(BF16)
        return dot(flat[:, :size], spread), keeper

    index = counter((1, features), 1)
    spread, keeper = unpack(index, own)
    spread = spread.reshape(owners, 8, features)
    keep = counter((owners, 8, features), 0) == keeper.reshape(1, 1, features)
    r.rows8[...] = jnp.sum(jnp.where(keep, spread, 0.0), axis=0)

    index = counter((1, 3 * width), 1)
    part = holder(index, width, 3)
    index = index + part * (features - width) + piece * width
    spread, keeper = unpack(index, 3 * own)
    keep = counter((owners * 8, 3 * width), 0) == keeper * 8 + 6
    r.bias_q[...] = jnp.sum(jnp.where(keep, spread, 0.0), axis=0, keepdims=True)
    index = counter((1, hidden), 1) + piece * hidden
    spread, keeper = unpack(index, v[7].shape[0])
    keep = counter((owners * 8, hidden), 0) == keeper * 8 + 7
    r.bias_u[...] = jnp.sum(jnp.where(keep, spread, 0.0), axis=0, keepdims=True)
    g_attn, b_attn, g_mlp, b_mlp = (r.rows8[n : n + 1, :] for n in range(4))

    attn_in, mlp_in = r.attn_in, r.mlp_in
    other_tokens(x_all, x_slots)

    def norm_step(j, carry):
        at = block(j, rows)
        data = x_all[at].astype(F32)
        mean = jnp.mean(data, axis=-1, keepdims=True)
        centered = data - mean
        inverse = lax.rsqrt(jnp.mean(centered * centered, axis=-1, keepdims=True) + EPSILON)
        r.mean[at] = mean
        r.inverse[at] = inverse
        unit = centered * inverse
        a = (unit * g_attn + b_attn).astype(BF16)
        m = (unit * g_mlp + b_mlp).astype(BF16)
        attn_in[at] = a
        mlp_in[at] = m
        r.attn_in_t[:, at] = a.T
        r.mlp_in_t[:, at] = m.T
        return carry

    lax.fori_loop(0, cores, norm_step, 0)

    half_rot = ROT // 2

    def turn(data, sign):
        seqs = data.shape[0] // SEQ
        cosine, back_sine, fore_sine = (
            jnp.concatenate([table[...]] * seqs, axis=0) if seqs > 1 else table[...]
            for table in (r.cosine, r.back_sine, r.fore_sine)
        )
        moved = (
            pltpu.roll(data, data.shape[1] - half_rot, 1) * back_sine
            + pltpu.roll(data, half_rot, 1) * fore_sine
        )
        return data * cosine + (moved if sign > 0 else -moved)

    wait_columns(wq, 0)

    def project_step(j, carry):
        at = block(j, pair)
        projected = dot(attn_in[at], wq[...]) + r.bias_q[...]
        r.q_s[at] = turn(projected[:, :width], 1).astype(BF16)
        r.k_s[at] = turn(projected[:, width : 2 * width], 1).astype(BF16)
        r.v_s[at] = projected[:, 2 * width :].astype(BF16)
        return carry

    lax.fori_loop(0, line, project_step, 0)

    lane = counter((SEQ, width), 1)

    def of_head(data, h):
        inside = (lane >= h * head_dim) & (lane < (h + 1) * head_dim)
        return jnp.where(inside, data, jnp.zeros_like(data))

    scale = head_dim ** (-0.5)

    def attend_step(s, carry):
        at = block(s, SEQ)
        queries, keys_rot, values = r.q_s[at], r.k_s[at], r.v_s[at]
        causal = counter((SEQ, SEQ), 0) >= counter((SEQ, SEQ), 1)
        total = jnp.zeros((SEQ, width), F32)
        for h in range(heads):
            scores = dot_last(of_head(queries, h), keys_rot) * scale
            scores = jnp.where(causal, scores, -jnp.inf)
            peak = jnp.max(scores, axis=-1, keepdims=True)
            logsum = peak + jnp.log(jnp.sum(jnp.exp(scores - peak), axis=-1, keepdims=True))
            probs = jnp.exp(scores - logsum)
            r.probs[s, h] = probs
            total = total + dot(probs.astype(BF16), of_head(values, h))
        context = total.astype(BF16)
        r.ctx[at] = context
        r.ctx_t[:, at] = context.T
        return carry

    lax.fori_loop(0, count // SEQ, attend_step, 0)

    pass_tokens(cot_all, cot_slots, relay_first)
    wait_columns(wu, 1)

    def hidden_step(j, carry):
        at = block(j, pair)
        pre = dot(mlp_in[at], wu[...]) + r.bias_u[...]
        chance = 0.5 * (1.0 + lax.erf(pre * SQRT_HALF))
        act = (pre * chance).astype(BF16)
        r.slope[at] = chance + pre * jnp.exp(-0.5 * pre * pre) * INV_ROOT_TAU
        r.act[at] = act
        r.act_t[:, at] = act.T
        return carry

    lax.fori_loop(0, line, hidden_step, 0)
    wp_wait()
    wd_wait()

    rows_in, rows_mid, rows_end = r.rows_in, r.rows_mid, r.rows_end
    swap_slot = net.slots(2 * line)
    end_slot = net.slots(2 * line)

    def swap(n, part, j):
        net.push(
            part.at[block(2 * j + 1 - c, rows)], rows_in.at[n, j], partner, swap_slot + n * line + j
        )

    relay_slot = net.slots(4)
    relay_in = r.relay_in
    end = (t == 0) | (t == line - 1) if line > 2 else None

    def send_sum(n, k):
        slot = end_slot + n * line + k
        to = me.on_line(k)
        net.push(rows_mid.at[n, to], rows_end.at[n, k], me.at(to, i, c), slot)

    def add_up(n, part):
        for k in [line - 1] + list(range(1, line - 1)) + [line] if line > 1 else [line]:
            to = me.on_line(k)
            net.arrived(rows_in.at[n, to], swap_slot + n * line + to)
            both = part[block(2 * to + c, rows)].astype(F32) + rows_in[n, to].astype(F32)
            rows_mid[n, to] = both.astype(BF16)
            if k == line:
                continue
            direct = jnp.bool_(True)
            far = me.ends(k)
            if far is not None:
                way = 0 if k == line - 1 else 1

                @pl.when(far)
                def _():
                    peer = me.at(line - 2 if k == 1 else 1, i, c)
                    slot = relay_slot + 2 * n + way
                    net.push(rows_mid.at[n, to], relay_in.at[n, way], peer, slot)

                direct = jnp.logical_not(far)
            net.later(rows_mid.at[n, to], [end_slot + n * line + k], direct)
            for at_k, at_t in adders:
                if k == at_k:
                    direct = jnp.logical_and(direct, t != at_t)
            pl.when(direct if end is None else jnp.logical_and(direct, jnp.logical_not(end)))(
                lambda: send_sum(n, k)
            )
        net.later(rows_in.at[n, 0], range(swap_slot + n * line, swap_slot + (n + 1) * line))

    def add_rest(n):
        if end is None:
            return

        @pl.when(end)
        def _():
            for way, last in enumerate((0, line - 1)):

                @pl.when(t == last)
                def _():
                    net.left(rows_mid.at[n, 0], relay_slot + 2 * n + way)

            for k in [2 % line] + [1, line - 1]:
                if k == 2 % line and k in (1, line - 1):
                    continue
                far = me.ends(k)
                send = lambda: send_sum(n, k)
                send() if far is None else pl.when(jnp.logical_not(far))(send)
            for k in range(3, line - 1):
                send_sum(n, k)

    def relay_up(n):
        for way, (k, at_t) in enumerate(adders):

            @pl.when(t == at_t)
            def _():
                to = me.on_line(k)
                net.arrived(relay_in.at[n, way], relay_slot + 2 * n + way)
                both = rows_mid[n, to].astype(F32) + relay_in[n, way].astype(F32)
                rows_mid[n, to] = both.astype(BF16)
                send_sum(n, k)

    def row_total(n):
        total = r.total
        total[...] = rows_mid[n, t].astype(F32)
        for k in range(1, line):

            def more():
                net.arrived(rows_end.at[n, k], end_slot + n * line + k)
                total[...] += rows_end[n, k].astype(F32)

            far = me.comes_far(k)
            more() if far is None else pl.when(jnp.logical_not(far))(more)
        return total[...]

    def out_step(j, carry):
        at = block(j, pair)
        part = dot(r.ctx[at], wp[...]) + dot(r.act[at], wd[...])
        r.out_part[at] = part.astype(BF16)
        swap(0, r.out_part, j)
        return carry

    lax.fori_loop(0, line, out_step, 0)
    add_up(0, r.out_part)

    pass_tokens(cot_all, cot_slots, relay_last)
    other_tokens(cot_all, cot_slots)

    def rows_back(source, landing):
        height = source.shape[0] // group
        half = height // 2
        slot = net.slots(2 * plane)
        for k in range(plane):
            to = me.in_plane(k)

            @pl.when(lax.div(to, group) == c)
            def _():
                for s in range(2):
                    src = source.at[
                        pl.ds(pl.multiple_of(lax.rem(to, group) * height + s * half, half), half)
                    ]
                    send = lambda: net.push(
                        src, landing.at[k], me.at(t, to, s), slot + 2 * k + s, slot + k
                    )
                    if k == 0:
                        pl.when(c == s)(lambda: net.local(src, landing.at[k], slot + k))
                        pl.when(c != s)(send)
                    else:
                        send()

        def arrive():
            for k in range(plane):
                net.arrived(landing.at[k], slot + k)

        def leave():
            for k in range(plane):
                to = me.in_plane(k)

                @pl.when(lax.div(to, group) == c)
                def _():
                    for s in range(2):
                        done = lambda: net.left(landing.at[k], slot + 2 * k + s)
                        if k == 0:
                            pl.when(c != s)(done)
                        else:
                            done()

        net.last.append(leave)
        return arrive

    def down_step(j, carry):
        at = block(j, LANES)
        r.gd[at] = dot(r.act_t[at], cot_all[...]).astype(BF16)
        return carry

    lax.fori_loop(0, hidden // LANES, down_step, 0)
    d_arrive = rows_back(r.gd, r.d_in)
    add_rest(0)
    relay_up(0)

    sums = r.sums
    sums[...] = jnp.zeros_like(sums)

    def slope_step(j, carry):
        at = block(j, pair)
        grad = dot_last(cot_all[at], wd[...]) * r.slope[at]
        sums[5:6, :hidden] += jnp.sum(grad, axis=0, keepdims=True)
        r.gpre[at] = grad.astype(BF16)
        r.gctx[at] = dot_last(cot_all[at], wp[...]).astype(BF16)
        return carry

    lax.fori_loop(0, line, slope_step, 0)

    q_in, u_in = r.q_in, r.u_in
    col_back = net.slots(2)

    def up_step(j, carry):
        grad = dot(r.mlp_in_t[block(j, span)], r.gpre[...]).astype(BF16)
        r.gu[j] = grad.reshape(plane, own, hidden)
        return carry

    lax.fori_loop(0, line, up_step, 0)
    for k in range(1, plane):
        to = me.in_plane(k)
        net.push(r.gu.at[:, to], u_in.at[k], me.at(t, to, c), col_back + 1)
    net.later(u_in.at[: plane - 1], [col_back + 1])

    def attend_back_step(s, carry):
        at = block(s, SEQ)
        queries, keys_rot, values, upper = r.q_s[at], r.k_s[at], r.v_s[at], r.gctx[at]
        g_queries = jnp.zeros((SEQ, width), F32)
        g_keys = jnp.zeros((SEQ, width), F32)
        g_values = jnp.zeros((SEQ, width), F32)
        for h in range(heads):
            probs = r.probs[s, h]
            upper_h = of_head(upper, h)
            g_probs = dot_last(upper_h, values)
            g_values = g_values + dot(probs.astype(BF16).T, upper_h)
            g_scores = (
                probs * (g_probs - jnp.sum(probs * g_probs, axis=-1, keepdims=True)) * scale
            ).astype(BF16)
            g_queries = g_queries + dot(g_scores, of_head(keys_rot, h))
            g_keys = g_keys + dot(g_scores.T, of_head(queries, h))
        parts = (turn(g_queries, -1), turn(g_keys, -1), g_values)
        for n, grad in enumerate(parts):
            lanes = slice(n * width, (n + 1) * width)
            sums[6:7, lanes] += jnp.sum(grad, axis=0, keepdims=True)
            r.gcol[at, lanes] = grad.astype(BF16)
        return carry

    lax.fori_loop(0, count // SEQ, attend_back_step, 0)

    def back_step(j, carry):
        at = block(j, pair)
        unit = (x_all[at].astype(F32) - r.mean[at]) * r.inverse[at]
        g_a = dot_last(r.gcol[at], wq[...])
        sums[0:1, :] += jnp.sum(g_a * unit, axis=0, keepdims=True)
        sums[1:2, :] += jnp.sum(g_a, axis=0, keepdims=True)
        g_m = dot_last(r.gpre[at], wu[...])
        sums[2:3, :] += jnp.sum(g_m * unit, axis=0, keepdims=True)
        sums[3:4, :] += jnp.sum(g_m, axis=0, keepdims=True)
        part = g_a * r.rows8[0:1, :] + g_m * r.rows8[2:3, :]
        r.back_part[at] = part.astype(BF16)
        swap(1, r.back_part, j)
        return carry

    lax.fori_loop(0, line, back_step, 0)
    add_up(1, r.back_part)
    sums[4:5, :] = jnp.sum(cot_all[mine].astype(F32), axis=0, keepdims=True)

    def qkv_step(j, carry):
        grad = dot(r.attn_in_t[block(j, span)], r.gcol[...]).astype(BF16)
        r.gq[j] = grad.reshape(plane, own, 3 * width)
        return carry

    lax.fori_loop(0, line, qkv_step, 0)
    for k in range(1, plane):
        to = me.in_plane(k)
        net.push(r.gq.at[:, to], q_in.at[k], me.at(t, to, c), col_back)
    net.later(q_in.at[: plane - 1], [col_back])
    add_rest(1)
    relay_up(1)
    r.gp[...] = dot(r.ctx_t[...], cot_all[...]).astype(BF16)
    p_arrive = rows_back(r.gp, r.p_in)

    sums_in, sums_all = r.sums_in, r.sums_all
    sum_slot = net.slots(1)
    for k in range(1, plane):
        net.push(sums, sums_in.at[k], me.at(t, me.in_plane(k), c), sum_slot)
    net.later(sums_in.at[: plane - 1], [sum_slot])

    q_mid, u_mid, q_end, u_end = r.q_mid, r.u_mid, r.q_end, r.u_end
    third = net.slots(2 * line)
    fourth = net.slots(2 * line)

    def column_total(n, source, landing, middle, end):
        net.arrived(landing.at[: plane - 1], col_back + n)
        for b in range(line):
            total = source[b, i].astype(F32)
            for k in range(1, plane):
                total = total + landing[k, b].astype(F32)
            middle[b] = total.astype(BF16)
        for k in range(1, line):
            to = me.on_line(k)
            net.push(middle.at[to], end.at[piece], me.at(to, i, c), third + 2 * k + n)
            net.later(middle.at[to], [third + 2 * k + n])
        end[piece] = middle[t]
        net.push(end.at[piece], end.at[piece], partner, fourth + n)
        net.later(end.at[piece], [fourth + 2 * k + n for k in range(line)])

    def column_pass(n, end):
        for k in range(1, line):
            ref = end.at[2 * me.on_line(-k) + c]
            net.arrived(ref, third + 2 * k + n)
            net.push(ref, ref, partner, fourth + 2 * k + n)

    def column_end(n, end):
        for k in range(line):
            net.arrived(end.at[2 * me.on_line(-k) + 1 - c], fourth + 2 * k + n)

    column_total(1, r.gu, u_in, u_mid, u_end)

    half_slot = net.slots(2)

    def row_end(n, landing, whole, arrive):
        arrive()
        half = landing.shape[1]
        total = landing[0].astype(F32)
        for k in range(1, plane):
            total = total + landing[k].astype(F32)
        at = whole.at[block(c, half)]
        at[...] = total
        net.push(at, at, partner, half_slot + n)
        net.later(at, [half_slot + n])

    row_end(0, r.d_in, r.gd_out, d_arrive)

    net.arrived(sums_in.at[: plane - 1], sum_slot)
    total = sums[...]
    for k in range(1, plane):
        total = total + sums_in[k]
    sums_all[piece] = total
    sum_second = net.slots(line)
    sum_third = net.slots(line)
    ref = sums_all.at[piece]
    for k in range(1, line):
        net.push(ref, ref, me.at(me.on_line(k), i, c), sum_second + k)
    net.push(ref, ref, partner, sum_third)
    net.later(ref, range(sum_second + 1, sum_second + line))
    net.later(ref, range(sum_third, sum_third + line))

    column_total(0, r.gq, q_in, q_mid, q_end)
    row_end(1, r.p_in, r.gp_out, p_arrive)

    for k in range(1, line):
        ref = sums_all.at[2 * me.on_line(-k) + c]
        net.arrived(ref, sum_second + k)
        net.push(ref, ref, partner, sum_third + k)
    column_pass(1, u_end)

    data = x_all[mine].astype(F32)
    bias = r.rows8[4:5, :] + r.rows8[5:6, :]
    r.output[...] = (data + row_total(0) + bias).astype(BF16)
    unit = (data - r.mean[mine]) * r.inverse[mine]
    grad = row_total(1)
    grad = r.inverse[mine] * (
        grad
        - jnp.mean(grad, axis=-1, keepdims=True)
        - unit * jnp.mean(grad * unit, axis=-1, keepdims=True)
    )
    r.grad_x[...] = (cot_all[mine].astype(F32) + grad).astype(BF16)

    column_pass(0, q_end)
    column_end(1, u_end)

    for k in range(line):
        net.arrived(sums_all.at[2 * me.on_line(-k) + 1 - c], sum_third + k)
    every = sums_all[...]
    total = every[0]
    for b in range(1, cores):
        total = total + every[b]
    chosen = counter((features, own), 0) == me.owner * own + counter((features, own), 1)
    r.five_out[...] = exact_dot(total, chosen.astype(F32))
    stacked = every.reshape(cores * 8, features)

    def pick(columns, size, keeper, column, row, out):
        chosen = (counter((columns, size), 0) == column).astype(F32)
        found = exact_dot(stacked[:, :columns], chosen)
        keep = counter((cores * 8, size), 0) == keeper * 8 + row
        out[...] = jnp.sum(jnp.where(keep, found, 0.0), axis=0, keepdims=True)

    size = v[7].shape[0]
    index = me.owner * size + counter((1, size), 1)
    keeper = holder(index, hidden, cores)
    pick(hidden, size, keeper, index - keeper * hidden, 5, r.bu_out)
    size = 3 * own
    index = me.owner * size + counter((1, size), 1)
    part = holder(index, features, 3)
    index = index - part * features
    keeper = holder(index, width, cores)
    pick(3 * width, size, keeper, index - keeper * width + part * width, 6, r.bq_out)

    column_end(0, q_end)
    for n, whole in enumerate((r.gd_out, r.gp_out)):
        half = whole.shape[0] // 2
        net.arrived(whole.at[block(1 - c, half)], half_slot + n)
    assert net.used <= r.send.shape[0]
    net.finish()


def finish_kernel(output, grad_x, q_end, u_end, gp, gd, five, bq, bu, *finals):
    (
        output_f,
        grad_x_f,
        gain_a,
        shift_a,
        gq_f,
        bq_f,
        gp_f,
        bp_f,
        gain_m,
        shift_m,
        gu_f,
        bu_f,
        gd_f,
        bd_f,
    ) = finals
    output_f[...] = output[...]
    grad_x_f[...] = grad_x[...]
    cores, _, hidden = u_end.shape
    width = q_end.shape[2] // 3
    for b in range(cores):
        gu_f[:, b * hidden : (b + 1) * hidden] = u_end[b].astype(F32)
        for part in range(3):
            at = (part * cores + b) * width
            gq_f[:, at : at + width] = q_end[b, :, part * width : (part + 1) * width].astype(F32)
    gp_f[...] = gp[...]
    gd_f[...] = gd[...]
    for n, leaf in enumerate((gain_a, shift_a, gain_m, shift_m, bp_f)):
        leaf[...] = five[n]
    bd_f[...] = five[4]
    bq_f[...] = bq[0]
    bu_f[...] = bu[0]


def turn_tables(width, head_dim):
    half = ROT // 2
    frequency = THETA ** (-2.0 * np.arange(half) / ROT)
    angles = np.arange(SEQ)[:, None] * frequency[None, :]
    cosine, sine = np.cos(angles), np.sin(angles)
    rest = head_dim - ROT
    heads = width // head_dim
    one = np.ones((SEQ, rest))
    none = np.zeros((SEQ, rest))
    zero = np.zeros((SEQ, half))
    tables = (
        [cosine, cosine, one],
        [-sine, zero, none],
        [zero, sine, none],
    )
    return [np.concatenate(parts * heads, axis=1).astype(np.float32) for parts in tables]


def local(
    inputs,
    cotangent,
    attn_gain,
    attn_shift,
    qkv_weight,
    qkv_bias,
    proj_weight,
    proj_bias,
    mlp_gain,
    mlp_shift,
    up_weight,
    up_bias,
    down_weight,
    down_bias,
):
    owners = lax.axis_size("fsdp")
    replicas = lax.axis_size("replica")
    rows, features = inputs.shape
    line, plane = degrees(owners, features)
    cores = 2 * line
    count = cores * rows
    head_dim = features // H
    width, hidden = features // cores, up_weight.shape[1] // cores
    own = features // owners
    proj_rows, down_rows = proj_weight.shape[0], down_weight.shape[0]
    heads = width // head_dim
    reach = -(-max(v.shape[0] for v in (attn_gain, qkv_bias, up_bias)) // LANES) * LANES

    vectors = (attn_gain, attn_shift, mlp_gain, mlp_shift, proj_bias, down_bias, qkv_bias, up_bias)
    outs = dict(
        output=((rows, features), BF16),
        grad_x=((rows, features), BF16),
        q_end=((cores, own, 3 * width), BF16),
        u_end=((cores, own, hidden), BF16),
        gp_out=((proj_rows, features), F32),
        gd_out=((down_rows, features), F32),
        five_out=((8, own), F32),
        bq_out=((1, 3 * own), F32),
        bu_out=((1, up_bias.shape[0]), F32),
    )
    tables = turn_tables(width, head_dim)
    scratch = dict(
        x_all=((count, features), BF16),
        cot_all=((count, features), BF16),
        wq=((features, 3 * width), BF16),
        wp=((width, features), BF16),
        wu=((features, hidden), BF16),
        wd=((hidden, features), BF16),
        vec_own=((8, reach), F32),
        vec_all=((owners, 8, reach), F32),
        rows8=((8, features), F32),
        bias_q=((1, 3 * width), F32),
        bias_u=((1, hidden), F32),
        mean=((count, 1), F32),
        inverse=((count, 1), F32),
        attn_in=((count, features), BF16),
        attn_in_t=((features, count), BF16),
        mlp_in=((count, features), BF16),
        mlp_in_t=((features, count), BF16),
        q_s=((count, width), BF16),
        k_s=((count, width), BF16),
        v_s=((count, width), BF16),
        probs=((count // SEQ, heads, SEQ, SEQ), F32),
        ctx=((count, width), BF16),
        ctx_t=((width, count), BF16),
        act=((count, hidden), BF16),
        act_t=((hidden, count), BF16),
        slope=((count, hidden), F32),
        gpre=((count, hidden), BF16),
        gcol=((count, 3 * width), BF16),
        gctx=((count, width), BF16),
        out_part=((count, features), BF16),
        back_part=((count, features), BF16),
        gq=((line, plane, own, 3 * width), BF16),
        gp=((width, features), BF16),
        gu=((line, plane, own, hidden), BF16),
        gd=((hidden, features), BF16),
        rows_in=((2, line, rows, features), BF16),
        rows_mid=((2, line, rows, features), BF16),
        rows_end=((2, line, rows, features), BF16),
        relay_in=((2, 2, rows, features), BF16),
        total=((rows, features), F32),
        q_in=((plane, line, own, 3 * width), BF16),
        u_in=((plane, line, own, hidden), BF16),
        q_mid=((line, own, 3 * width), BF16),
        u_mid=((line, own, hidden), BF16),
        p_in=((plane, proj_rows // 2, features), BF16),
        d_in=((plane, down_rows // 2, features), BF16),
        sums=((8, features), F32),
        sums_in=((plane, 8, features), F32),
        sums_all=((cores, 8, features), F32),
    )
    scratch.update(zip(("v%d" % n for n in range(8)), ((v.shape, BF16) for v in vectors)))
    scratch.update(
        cosine=((SEQ, width), F32), back_sine=((SEQ, width), F32), fore_sine=((SEQ, width), F32)
    )
    operands = (inputs, cotangent, qkv_weight, proj_weight, up_weight, down_weight, *vectors, *tables)
    operands = [pltpu.with_memory_space_constraint(a, pltpu.HBM) for a in operands]
    sems = 20 + 18 * line + 10 * plane
    vmem = pl.BlockSpec(memory_space=pltpu.VMEM)
    results = pl.pallas_call(
        functools.partial(layer_kernel, line, plane, head_dim, list(outs) + list(scratch)),
        out_shape=[jax.ShapeDtypeStruct(*outs[name]) for name in outs],
        in_specs=[pl.BlockSpec(memory_space=pltpu.HBM)] * 17,
        out_specs=[vmem] * len(outs),
        scratch_shapes=[pltpu.VMEM(*scratch[name]) for name in scratch]
        + [pltpu.SemaphoreType.DMA((sems,)), pltpu.SemaphoreType.DMA((sems,))],
        compiler_params=pltpu.CompilerParams(
            collective_id=0, has_side_effects=True, vmem_limit_bytes=VMEM_BYTES
        ),
        name="layer",
    )(*operands)
    gradients = (
        ((own,), F32),
        ((own,), F32),
        ((own, 3 * features), F32),
        ((3 * own,), F32),
        ((proj_rows, features), F32),
        ((own,), F32),
        ((own,), F32),
        ((own,), F32),
        ((own, cores * hidden), F32),
        (up_bias.shape, F32),
        ((down_rows, features), F32),
        ((own,), F32),
    )
    final = tuple(outs.values())[:2] + gradients
    final = pl.pallas_call(
        finish_kernel,
        out_shape=[jax.ShapeDtypeStruct(*leaf) for leaf in final],
        in_specs=[vmem] * len(outs),
        out_specs=[vmem] * len(final),
        compiler_params=pltpu.CompilerParams(vmem_limit_bytes=VMEM_BYTES),
        name="finish",
    )(*results)
    final = list(final)
    if replicas > 2:
        groups = [[j for j in range(replicas) if j % 2 == k] for k in range(2)]
        final[2:] = lax.psum(tuple(final[2:]), "replica", axis_index_groups=groups)
    return tuple(final)


def solution(mesh):
    return jax.shard_map(
        local,
        mesh=mesh,
        in_specs=(
            P(("fsdp", "replica"), None),
            P(("fsdp", "replica"), None),
            P("fsdp"),
            P("fsdp"),
            P("fsdp", None),
            P("fsdp"),
            P("fsdp", None),
            P("fsdp"),
            P("fsdp"),
            P("fsdp"),
            P("fsdp", None),
            P("fsdp"),
            P("fsdp", None),
            P("fsdp"),
        ),
        out_specs=(
            P(("fsdp", "replica"), None),
            P(("fsdp", "replica"), None),
            P("fsdp"),
            P("fsdp"),
            P("fsdp", None),
            P("fsdp"),
            P("fsdp", None),
            P("fsdp"),
            P("fsdp"),
            P("fsdp"),
            P("fsdp", None),
            P("fsdp"),
            P("fsdp", None),
            P("fsdp"),
        ),
        check_vma=False,
    )
```

```python
import functools
import math

import jax
import jax.numpy as jnp
import numpy as np
from jax import lax
from jax.experimental import pallas as pl
from jax.experimental.pallas import tpu as pltpu
from jax.sharding import PartitionSpec as P

H = 16
ROT = 16
SEQ = 128


EPSILON = 1e-05
THETA = 10000.0
SQRT_HALF = 0.7071067811865476
INV_ROOT_TAU = 0.3989422804014327


MESH = pl.DeviceIdType.MESH
LANES = 128
BF16 = jnp.bfloat16
F32 = jnp.float32
VMEM_BYTES = 48 * 1024 * 1024


def degrees(owners, features):
    line = math.gcd(owners, features // (2 * LANES))
    return line, owners // line


class Place:
    def __init__(self, line, plane):
        self.line, self.plane = line, plane
        self.owner = lax.axis_index("fsdp")
        replica = lax.axis_index("replica")
        self.t = lax.div(self.owner, plane)
        self.i = lax.rem(self.owner, plane)
        self.c = lax.rem(replica, 2)
        self.base = replica - self.c

    def at(self, t, i, c):
        return (t * self.plane + i, self.base + c)

    def on_line(self, k):
        return lax.rem(self.t + (k + self.line), self.line)

    def in_plane(self, k):
        return lax.rem(self.i + (k + self.plane), self.plane)

    def ends(self, k):
        if self.line < 3 or k not in (1, self.line - 1):
            return None
        return self.t == (0 if k == self.line - 1 else self.line - 1)

    def comes_far(self, k):
        if self.line < 3 or k not in (1, self.line - 1):
            return None
        return self.t == (self.line - 1 if k == self.line - 1 else 0)

    def greet(self):
        barrier = pltpu.get_barrier_semaphore()
        peers = [self.at(self.on_line(k), self.i, self.c) for k in range(1, self.line)]
        peers += [self.at(self.t, self.in_plane(k), self.c) for k in range(1, self.plane)]
        peers += [self.at(self.t, self.in_plane(k), 1 - self.c) for k in range(self.plane)]
        for peer in peers:
            pl.semaphore_signal(barrier, inc=1, device_id=peer, device_id_type=MESH)
        pl.semaphore_wait(barrier, len(peers))


class Copies:
    def __init__(self, send, recv):
        self.send, self.recv = send, recv
        self.used = 0
        self.last = []

    def slots(self, count):
        first = self.used
        self.used += count
        return first

    def push(self, src, dst, peer, slot, land=None):
        pltpu.make_async_remote_copy(
            src_ref=src,
            dst_ref=dst,
            send_sem=self.send.at[slot],
            recv_sem=self.recv.at[slot if land is None else land],
            device_id=peer,
            device_id_type=MESH,
        ).start()

    def local(self, src, dst, slot):
        pltpu.make_async_copy(src, dst, self.recv.at[slot]).start()

    def arrived(self, ref, slot):
        pltpu.make_async_copy(ref, ref, self.recv.at[slot]).wait()

    def left(self, ref, slot):
        pltpu.make_async_copy(ref, ref, self.send.at[slot]).wait()

    def later(self, ref, slots, when=None):
        def done():
            for slot in slots:
                self.left(ref, slot)

        self.last.append(done if when is None else lambda: pl.when(when)(done))

    def finish(self):
        for done in self.last:
            done()


def block(index, size):
    return pl.ds(pl.multiple_of(index * size, size), size)


def dot(left, right):
    return jnp.dot(left, right, preferred_element_type=F32)


def dot_last(left, right):
    return lax.dot_general(left, right, (((1,), (1,)), ((), ())), preferred_element_type=F32)


def exact_dot(left, right):
    return jnp.dot(left, right, preferred_element_type=F32, precision=lax.Precision.HIGHEST)


def counter(dims, axis):
    return lax.broadcasted_iota(jnp.int32, dims, axis)


def holder(index, width, count):
    found = jnp.zeros_like(index)
    for k in range(1, count):
        found = found + (index >= k * width).astype(jnp.int32)
    return found


class Refs:
    def __init__(self, refs, named):
        self.x, self.cot, self.wqkv, self.wproj, self.wup, self.wdown = refs[:6]
        self.small = refs[6:17]
        self.send, self.recv = refs[-2:]
        self.__dict__.update(zip(named, refs[17:-2]))


def layer_kernel(line, plane, head_dim, named, *refs):
    r = Refs(refs, named)
    me = Place(line, plane)
    t, i, c = me.t, me.i, me.c
    net = Copies(r.send, r.recv)
    owners, cores, group = line * plane, 2 * line, plane // 2
    x, cot, wqkv, wup = r.x, r.cot, r.wqkv, r.wup
    x_all, cot_all, wq, wp, wu, wd = r.x_all, r.cot_all, r.wq, r.wp, r.wu, r.wd
    rows, features = x.shape
    count = cores * rows
    pair = 2 * rows
    width = features // cores
    hidden = wup.shape[1] // cores
    own = features // owners
    span = features // line
    heads = width // head_dim
    piece = 2 * t + c
    mine = block(piece, rows)
    partner = me.at(t, i, 1 - c)
    small = [r.v0, r.v1, r.v2, r.v3, r.v4, r.v5, r.v6, r.v7, r.cosine, r.back_sine, r.fore_sine]
    v = small[:8]
    vec_own, vec_all = r.vec_own, r.vec_all
    reach = vec_own.shape[1]

    relays, adders = [], []
    if line > 2:
        adders = [(line - 2, 1), (2 % line, line - 2)]
        relays = [(line - 2, line - 2, 1, line - 1), (2 % line, 1, -1, 1)]
    relay_first = sorted({at_k for at_k, *_ in relays})
    relay_last = [k for k in range(1, line) if k not in relay_first]

    small_slot = net.slots(len(small))
    for n, ref in enumerate(small):
        net.local(r.small[n], ref, small_slot + n)
    me.greet()
    for n, ref in enumerate(small):
        net.arrived(ref, small_slot + n)

    vec_own[...] = jnp.zeros_like(vec_own)
    for n in range(8):
        size = v[n].shape[0]
        vec_own[n : n + 1, :size] = v[n][...].astype(F32).reshape(1, size)
    vec_all[me.owner] = vec_own[...]
    vec_first = net.slots(1)
    for k in range(1, plane):
        net.push(vec_own, vec_all.at[me.owner], me.at(t, me.in_plane(k), c), vec_first)
    net.later(vec_all.at[: plane - 1], [vec_first])

    col_slot = net.slots(2 * line)
    shard = pl.ds(pl.multiple_of(t * span + i * own, own), own)
    def move(k, n, src, dst):
        slot = col_slot + 2 * k + n
        if k == 0:
            net.local(src, dst, slot)
        else:
            net.push(src, dst, me.at(me.on_line(k), i, c), slot)

    for k in range(line):
        for part in range(3):
            at = (part * cores + 2 * me.on_line(k) + c) * width
            src = wqkv.at[:, pl.ds(pl.multiple_of(at, LANES), width)]
            move(k, 0, src, wq.at[shard, part * width : (part + 1) * width])

    def send_tokens(src, whole):
        line_slot = net.slots(line)
        pair_slot = net.slots(line)
        pass_slot = net.slots(2)
        for k in relay_first + relay_last:
            far = me.ends(k)
            near = None if far is None else jnp.logical_not(far)
            send = lambda: net.push(
                src, whole.at[mine], me.at(me.on_line(k), i, c), line_slot + k
            )
            net.later(whole.at[mine], [line_slot + k], near)
            for _, at_t, _, land in relays if line > 3 else []:
                if k == land:
                    ready = t != at_t
                    near = ready if near is None else jnp.logical_and(near, ready)
            send() if near is None else pl.when(near)(send)
        net.local(src, whole.at[mine], line_slot)
        net.push(src, whole.at[mine], partner, pair_slot)
        net.later(whole.at[mine], range(pair_slot, pair_slot + line))
        return line_slot, pair_slot, pass_slot, src

    def pass_tokens(whole, slots, distances):
        line_slot, pair_slot, pass_slot, src = slots
        for k in distances:
            ref = whole.at[block(2 * me.on_line(-k) + c, rows)]
            net.arrived(ref, line_slot + k)
            for n, (at_k, at_t, step, land) in enumerate(relays):
                if k == at_k:

                    @pl.when(t == at_t)
                    def _():
                        peer = me.at(me.on_line(step), i, c)
                        net.push(ref, ref, peer, pass_slot + n, line_slot + land)
                        if line > 3:
                            peer = me.at(me.on_line(-step), i, c)
                            net.push(src, whole.at[mine], peer, line_slot + land)

                    net.later(ref, [pass_slot + n], t == at_t)
            net.push(ref, ref, partner, pair_slot + k)

    def other_tokens(whole, slots):
        for k in range(line):
            net.arrived(whole.at[block(2 * me.on_line(-k) + 1 - c, rows)], slots[1] + k)
        net.arrived(whole.at[mine], slots[0])

    x_slots = send_tokens(x, x_all)
    for k in range(line):
        move(k, 1, wup.at[:, block(2 * me.on_line(k) + c, hidden)], wu.at[shard])

    def rows_out(source, whole):
        height = source.shape[0]
        half = height // 2
        core = lax.div(i, group)
        src = source.at[block(c, half)]
        dst = whole.at[
            pl.ds(pl.multiple_of(lax.rem(i, group) * height + c * half, half), half)
        ]
        first = net.slots(2 * plane)
        away = net.slots(plane)
        for k in range(1, plane):
            net.push(src, dst, me.at(t, me.in_plane(k), core), away + k, first + 2 * k + c)
        net.later(dst, range(away + 1, away + plane))

        @pl.when(core == c)
        def _():
            net.local(src, dst, first + c)

        @pl.when(core != c)
        def _():
            net.push(src, dst, me.at(t, i, core), away, first + c)

        net.last.append(lambda: pl.when(core != c)(lambda: net.left(dst, away)))

        def wait():
            for k in range(plane):
                origin = me.in_plane(-k)

                @pl.when(lax.div(origin, group) == c)
                def _():
                    for s in range(2):
                        at = lax.rem(origin, group) * height + s * half
                        net.arrived(
                            whole.at[pl.ds(pl.multiple_of(at, half), half)], first + 2 * k + s
                        )

        return wait

    wp_wait = rows_out(r.wproj, wp)
    wd_wait = rows_out(r.wdown, wd)

    onward = net.slots(2)

    def strip(source, owner):
        return pl.ds(pl.multiple_of(source * span + owner * own, own), own)

    net.arrived(vec_all.at[: plane - 1], vec_first)
    vec_second = net.slots(1)
    bundle = vec_all.at[pl.ds(t * plane, plane)]
    for k in range(1, line):
        net.push(bundle, bundle, me.at(me.on_line(k), i, c), vec_second)
    others = vec_all.at[: (line - 1) * plane]
    if line > 1:
        net.later(others, [vec_second])

    def columns_on(whole, n):
        for k in range(line):
            at = strip(me.on_line(-k), i)
            net.arrived(whole.at[at], col_slot + 2 * k + n)
            if k > 0:
                net.later(whole.at[at], [col_slot + 2 * k + n])
            for j in range(1, plane):
                net.push(whole.at[at], whole.at[at], me.at(t, me.in_plane(j), c), onward + n)
        net.later(whole.at[: line * (plane - 1) * own], [onward + n])

    columns_on(wq, 0)
    columns_on(wu, 1)

    def wait_columns(whole, n):
        net.arrived(whole.at[: line * (plane - 1) * own], onward + n)

    pass_tokens(x_all, x_slots, relay_first + relay_last)
    cot_slots = send_tokens(cot, cot_all)

    if line > 1:
        net.arrived(others, vec_second)
    flat = vec_all[...].reshape(owners * 8, reach).astype(BF16)

    def unpack(index, size):
        keeper = holder(index, size, owners)
        spread = (counter((size, index.shape[1]), 0) == index - keeper * size).astype(BF16)
        return dot(flat[:, :size], spread), keeper

    index = counter((1, features), 1)
    spread, keeper = unpack(index, own)
    spread = spread.reshape(owners, 8, features)
    keep = counter((owners, 8, features), 0) == keeper.reshape(1, 1, features)
    r.rows8[...] = jnp.sum(jnp.where(keep, spread, 0.0), axis=0)

    index = counter((1, 3 * width), 1)
    part = holder(index, width, 3)
    index = index + part * (features - width) + piece * width
    spread, keeper = unpack(index, 3 * own)
    keep = counter((owners * 8, 3 * width), 0) == keeper * 8 + 6
    r.bias_q[...] = jnp.sum(jnp.where(keep, spread, 0.0), axis=0, keepdims=True)
    index = counter((1, hidden), 1) + piece * hidden
    spread, keeper = unpack(index, v[7].shape[0])
    keep = counter((owners * 8, hidden), 0) == keeper * 8 + 7
    r.bias_u[...] = jnp.sum(jnp.where(keep, spread, 0.0), axis=0, keepdims=True)
    g_attn, b_attn, g_mlp, b_mlp = (r.rows8[n : n + 1, :] for n in range(4))

    attn_in, mlp_in = r.attn_in, r.mlp_in
    other_tokens(x_all, x_slots)

    def norm_step(j, carry):
        at = block(j, rows)
        data = x_all[at].astype(F32)
        mean = jnp.mean(data, axis=-1, keepdims=True)
        centered = data - mean
        inverse = lax.rsqrt(jnp.mean(centered * centered, axis=-1, keepdims=True) + EPSILON)
        r.mean[at] = mean
        r.inverse[at] = inverse
        unit = centered * inverse
        a = (unit * g_attn + b_attn).astype(BF16)
        m = (unit * g_mlp + b_mlp).astype(BF16)
        attn_in[at] = a
        mlp_in[at] = m
        r.attn_in_t[:, at] = a.T
        r.mlp_in_t[:, at] = m.T
        return carry

    lax.fori_loop(0, cores, norm_step, 0)

    half_rot = ROT // 2

    def turn(data, sign):
        seqs = data.shape[0] // SEQ
        cosine, back_sine, fore_sine = (
            jnp.concatenate([table[...]] * seqs, axis=0) if seqs > 1 else table[...]
            for table in (r.cosine, r.back_sine, r.fore_sine)
        )
        moved = (
            pltpu.roll(data, data.shape[1] - half_rot, 1) * back_sine
            + pltpu.roll(data, half_rot, 1) * fore_sine
        )
        return data * cosine + (moved if sign > 0 else -moved)

    wait_columns(wq, 0)

    def project_step(j, carry):
        at = block(j, pair)
        projected = dot(attn_in[at], wq[...]) + r.bias_q[...]
        r.q_s[at] = turn(projected[:, :width], 1).astype(BF16)
        r.k_s[at] = turn(projected[:, width : 2 * width], 1).astype(BF16)
        r.v_s[at] = projected[:, 2 * width :].astype(BF16)
        return carry

    lax.fori_loop(0, line, project_step, 0)

    lane = counter((SEQ, width), 1)

    def of_head(data, h):
        inside = (lane >= h * head_dim) & (lane < (h + 1) * head_dim)
        return jnp.where(inside, data, jnp.zeros_like(data))

    scale = head_dim ** (-0.5)

    def attend_step(s, carry):
        at = block(s, SEQ)
        queries, keys_rot, values = r.q_s[at], r.k_s[at], r.v_s[at]
        causal = counter((SEQ, SEQ), 0) >= counter((SEQ, SEQ), 1)
        total = jnp.zeros((SEQ, width), F32)
        for h in range(heads):
            scores = dot_last(of_head(queries, h), keys_rot) * scale
            scores = jnp.where(causal, scores, -jnp.inf)
            peak = jnp.max(scores, axis=-1, keepdims=True)
            logsum = peak + jnp.log(jnp.sum(jnp.exp(scores - peak), axis=-1, keepdims=True))
            probs = jnp.exp(scores - logsum)
            r.probs[s, h] = probs
            total = total + dot(probs.astype(BF16), of_head(values, h))
        context = total.astype(BF16)
        r.ctx[at] = context
        r.ctx_t[:, at] = context.T
        return carry

    lax.fori_loop(0, count // SEQ, attend_step, 0)

    pass_tokens(cot_all, cot_slots, relay_first)
    wait_columns(wu, 1)

    def hidden_step(j, carry):
        at = block(j, pair)
        pre = dot(mlp_in[at], wu[...]) + r.bias_u[...]
        chance = 0.5 * (1.0 + lax.erf(pre * SQRT_HALF))
        act = (pre * chance).astype(BF16)
        r.slope[at] = chance + pre * jnp.exp(-0.5 * pre * pre) * INV_ROOT_TAU
        r.act[at] = act
        r.act_t[:, at] = act.T
        return carry

    lax.fori_loop(0, line, hidden_step, 0)
    wp_wait()
    wd_wait()

    rows_in, rows_mid, rows_end = r.rows_in, r.rows_mid, r.rows_end
    swap_slot = net.slots(2 * line)
    end_slot = net.slots(2 * line)

    def swap(n, part, j):
        net.push(
            part.at[block(2 * j + 1 - c, rows)], rows_in.at[n, j], partner, swap_slot + n * line + j
        )

    relay_slot = net.slots(4)
    relay_in = r.relay_in
    end = (t == 0) | (t == line - 1) if line > 2 else None

    def send_sum(n, k):
        slot = end_slot + n * line + k
        to = me.on_line(k)
        net.push(rows_mid.at[n, to], rows_end.at[n, k], me.at(to, i, c), slot)

    def add_up(n, part):
        for k in [line - 1] + list(range(1, line - 1)) + [line] if line > 1 else [line]:
            to = me.on_line(k)
            net.arrived(rows_in.at[n, to], swap_slot + n * line + to)
            both = part[block(2 * to + c, rows)].astype(F32) + rows_in[n, to].astype(F32)
            rows_mid[n, to] = both.astype(BF16)
            if k == line:
                continue
            direct = jnp.bool_(True)
            far = me.ends(k)
            if far is not None:
                way = 0 if k == line - 1 else 1

                @pl.when(far)
                def _():
                    peer = me.at(line - 2 if k == 1 else 1, i, c)
                    slot = relay_slot + 2 * n + way
                    net.push(rows_mid.at[n, to], relay_in.at[n, way], peer, slot)

                direct = jnp.logical_not(far)
            net.later(rows_mid.at[n, to], [end_slot + n * line + k], direct)
            for at_k, at_t in adders:
                if k == at_k:
                    direct = jnp.logical_and(direct, t != at_t)
            pl.when(direct if end is None else jnp.logical_and(direct, jnp.logical_not(end)))(
                lambda: send_sum(n, k)
            )
        net.later(rows_in.at[n, 0], range(swap_slot + n * line, swap_slot + (n + 1) * line))

    def add_rest(n):
        if end is None:
            return

        @pl.when(end)
        def _():
            for way, last in enumerate((0, line - 1)):

                @pl.when(t == last)
                def _():
                    net.left(rows_mid.at[n, 0], relay_slot + 2 * n + way)

            for k in [2 % line] + [1, line - 1]:
                if k == 2 % line and k in (1, line - 1):
                    continue
                far = me.ends(k)
                send = lambda: send_sum(n, k)
                send() if far is None else pl.when(jnp.logical_not(far))(send)
            for k in range(3, line - 1):
                send_sum(n, k)

    def relay_up(n):
        for way, (k, at_t) in enumerate(adders):

            @pl.when(t == at_t)
            def _():
                to = me.on_line(k)
                net.arrived(relay_in.at[n, way], relay_slot + 2 * n + way)
                both = rows_mid[n, to].astype(F32) + relay_in[n, way].astype(F32)
                rows_mid[n, to] = both.astype(BF16)
                send_sum(n, k)

    def row_total(n):
        total = r.total
        total[...] = rows_mid[n, t].astype(F32)
        for k in range(1, line):

            def more():
                net.arrived(rows_end.at[n, k], end_slot + n * line + k)
                total[...] += rows_end[n, k].astype(F32)

            far = me.comes_far(k)
            more() if far is None else pl.when(jnp.logical_not(far))(more)
        return total[...]

    def out_step(j, carry):
        at = block(j, pair)
        part = dot(r.ctx[at], wp[...]) + dot(r.act[at], wd[...])
        r.out_part[at] = part.astype(BF16)
        swap(0, r.out_part, j)
        return carry

    lax.fori_loop(0, line, out_step, 0)
    add_up(0, r.out_part)

    pass_tokens(cot_all, cot_slots, relay_last)
    other_tokens(cot_all, cot_slots)

    def rows_back(source, landing):
        height = source.shape[0] // group
        half = height // 2
        slot = net.slots(2 * plane)
        for k in range(plane):
            to = me.in_plane(k)

            @pl.when(lax.div(to, group) == c)
            def _():
                for s in range(2):
                    src = source.at[
                        pl.ds(pl.multiple_of(lax.rem(to, group) * height + s * half, half), half)
                    ]
                    send = lambda: net.push(
                        src, landing.at[k], me.at(t, to, s), slot + 2 * k + s, slot + k
                    )
                    if k == 0:
                        pl.when(c == s)(lambda: net.local(src, landing.at[k], slot + k))
                        pl.when(c != s)(send)
                    else:
                        send()

        def arrive():
            for k in range(plane):
                net.arrived(landing.at[k], slot + k)

        def leave():
            for k in range(plane):
                to = me.in_plane(k)

                @pl.when(lax.div(to, group) == c)
                def _():
                    for s in range(2):
                        done = lambda: net.left(landing.at[k], slot + 2 * k + s)
                        if k == 0:
                            pl.when(c != s)(done)
                        else:
                            done()

        net.last.append(leave)
        return arrive

    def down_step(j, carry):
        at = block(j, LANES)
        r.gd[at] = dot(r.act_t[at], cot_all[...]).astype(BF16)
        return carry

    lax.fori_loop(0, hidden // LANES, down_step, 0)
    d_arrive = rows_back(r.gd, r.d_in)
    add_rest(0)
    relay_up(0)

    sums = r.sums
    sums[...] = jnp.zeros_like(sums)

    def slope_step(j, carry):
        at = block(j, pair)
        grad = dot_last(cot_all[at], wd[...]) * r.slope[at]
        sums[5:6, :hidden] += jnp.sum(grad, axis=0, keepdims=True)
        r.gpre[at] = grad.astype(BF16)
        r.gctx[at] = dot_last(cot_all[at], wp[...]).astype(BF16)
        return carry

    lax.fori_loop(0, line, slope_step, 0)

    q_in, u_in = r.q_in, r.u_in
    col_back = net.slots(2)

    def up_step(j, carry):
        grad = dot(r.mlp_in_t[block(j, span)], r.gpre[...]).astype(BF16)
        r.gu[j] = grad.reshape(plane, own, hidden)
        return carry

    lax.fori_loop(0, line, up_step, 0)
    for k in range(1, plane):
        to = me.in_plane(k)
        net.push(r.gu.at[:, to], u_in.at[k], me.at(t, to, c), col_back + 1)
    net.later(u_in.at[: plane - 1], [col_back + 1])

    def attend_back_step(s, carry):
        at = block(s, SEQ)
        queries, keys_rot, values, upper = r.q_s[at], r.k_s[at], r.v_s[at], r.gctx[at]
        g_queries = jnp.zeros((SEQ, width), F32)
        g_keys = jnp.zeros((SEQ, width), F32)
        g_values = jnp.zeros((SEQ, width), F32)
        for h in range(heads):
            probs = r.probs[s, h]
            upper_h = of_head(upper, h)
            g_probs = dot_last(upper_h, values)
            g_values = g_values + dot(probs.astype(BF16).T, upper_h)
            g_scores = (
                probs * (g_probs - jnp.sum(probs * g_probs, axis=-1, keepdims=True)) * scale
            ).astype(BF16)
            g_queries = g_queries + dot(g_scores, of_head(keys_rot, h))
            g_keys = g_keys + dot(g_scores.T, of_head(queries, h))
        parts = (turn(g_queries, -1), turn(g_keys, -1), g_values)
        for n, grad in enumerate(parts):
            lanes = slice(n * width, (n + 1) * width)
            sums[6:7, lanes] += jnp.sum(grad, axis=0, keepdims=True)
            r.gcol[at, lanes] = grad.astype(BF16)
        return carry

    lax.fori_loop(0, count // SEQ, attend_back_step, 0)

    def back_step(j, carry):
        at = block(j, pair)
        unit = (x_all[at].astype(F32) - r.mean[at]) * r.inverse[at]
        g_a = dot_last(r.gcol[at], wq[...])
        sums[0:1, :] += jnp.sum(g_a * unit, axis=0, keepdims=True)
        sums[1:2, :] += jnp.sum(g_a, axis=0, keepdims=True)
        g_m = dot_last(r.gpre[at], wu[...])
        sums[2:3, :] += jnp.sum(g_m * unit, axis=0, keepdims=True)
        sums[3:4, :] += jnp.sum(g_m, axis=0, keepdims=True)
        part = g_a * r.rows8[0:1, :] + g_m * r.rows8[2:3, :]
        r.back_part[at] = part.astype(BF16)
        swap(1, r.back_part, j)
        return carry

    lax.fori_loop(0, line, back_step, 0)
    add_up(1, r.back_part)
    sums[4:5, :] = jnp.sum(cot_all[mine].astype(F32), axis=0, keepdims=True)

    def qkv_step(j, carry):
        grad = dot(r.attn_in_t[block(j, span)], r.gcol[...]).astype(BF16)
        r.gq[j] = grad.reshape(plane, own, 3 * width)
        return carry

    lax.fori_loop(0, line, qkv_step, 0)
    for k in range(1, plane):
        to = me.in_plane(k)
        net.push(r.gq.at[:, to], q_in.at[k], me.at(t, to, c), col_back)
    net.later(q_in.at[: plane - 1], [col_back])
    add_rest(1)
    relay_up(1)
    r.gp[...] = dot(r.ctx_t[...], cot_all[...]).astype(BF16)
    p_arrive = rows_back(r.gp, r.p_in)

    sums_in, sums_all = r.sums_in, r.sums_all
    sum_slot = net.slots(1)
    for k in range(1, plane):
        net.push(sums, sums_in.at[k], me.at(t, me.in_plane(k), c), sum_slot)
    net.later(sums_in.at[: plane - 1], [sum_slot])

    q_mid, u_mid, q_end, u_end = r.q_mid, r.u_mid, r.q_end, r.u_end
    third = net.slots(2 * line)
    fourth = net.slots(2 * line)

    def column_total(n, source, landing, middle, end):
        net.arrived(landing.at[: plane - 1], col_back + n)
        for b in range(line):
            total = source[b, i].astype(F32)
            for k in range(1, plane):
                total = total + landing[k, b].astype(F32)
            middle[b] = total.astype(BF16)
        for k in range(1, line):
            to = me.on_line(k)
            net.push(middle.at[to], end.at[piece], me.at(to, i, c), third + 2 * k + n)
            net.later(middle.at[to], [third + 2 * k + n])
        end[piece] = middle[t]
        net.push(end.at[piece], end.at[piece], partner, fourth + n)
        net.later(end.at[piece], [fourth + 2 * k + n for k in range(line)])

    def column_pass(n, end):
        for k in range(1, line):
            ref = end.at[2 * me.on_line(-k) + c]
            net.arrived(ref, third + 2 * k + n)
            net.push(ref, ref, partner, fourth + 2 * k + n)

    def column_end(n, end):
        for k in range(line):
            net.arrived(end.at[2 * me.on_line(-k) + 1 - c], fourth + 2 * k + n)

    column_total(1, r.gu, u_in, u_mid, u_end)

    half_slot = net.slots(2)

    def row_end(n, landing, whole, arrive):
        arrive()
        half = landing.shape[1]
        total = landing[0].astype(F32)
        for k in range(1, plane):
            total = total + landing[k].astype(F32)
        at = whole.at[block(c, half)]
        at[...] = total
        net.push(at, at, partner, half_slot + n)
        net.later(at, [half_slot + n])

    row_end(0, r.d_in, r.gd_out, d_arrive)

    net.arrived(sums_in.at[: plane - 1], sum_slot)
    total = sums[...]
    for k in range(1, plane):
        total = total + sums_in[k]
    sums_all[piece] = total
    sum_second = net.slots(line)
    sum_third = net.slots(line)
    ref = sums_all.at[piece]
    for k in range(1, line):
        net.push(ref, ref, me.at(me.on_line(k), i, c), sum_second + k)
    net.push(ref, ref, partner, sum_third)
    net.later(ref, range(sum_second + 1, sum_second + line))
    net.later(ref, range(sum_third, sum_third + line))

    column_total(0, r.gq, q_in, q_mid, q_end)
    row_end(1, r.p_in, r.gp_out, p_arrive)

    for k in range(1, line):
        ref = sums_all.at[2 * me.on_line(-k) + c]
        net.arrived(ref, sum_second + k)
        net.push(ref, ref, partner, sum_third + k)
    column_pass(1, u_end)

    data = x_all[mine].astype(F32)
    bias = r.rows8[4:5, :] + r.rows8[5:6, :]
    r.output[...] = (data + row_total(0) + bias).astype(BF16)
    unit = (data - r.mean[mine]) * r.inverse[mine]
    grad = row_total(1)
    grad = r.inverse[mine] * (
        grad
        - jnp.mean(grad, axis=-1, keepdims=True)
        - unit * jnp.mean(grad * unit, axis=-1, keepdims=True)
    )
    r.grad_x[...] = (cot_all[mine].astype(F32) + grad).astype(BF16)

    column_pass(0, q_end)
    column_end(1, u_end)

    for k in range(line):
        net.arrived(sums_all.at[2 * me.on_line(-k) + 1 - c], sum_third + k)
    every = sums_all[...]
    total = every[0]
    for b in range(1, cores):
        total = total + every[b]
    chosen = counter((features, own), 0) == me.owner * own + counter((features, own), 1)
    r.five_out[...] = exact_dot(total, chosen.astype(F32))
    stacked = every.reshape(cores * 8, features)

    def pick(columns, size, keeper, column, row, out):
        chosen = (counter((columns, size), 0) == column).astype(F32)
        found = exact_dot(stacked[:, :columns], chosen)
        keep = counter((cores * 8, size), 0) == keeper * 8 + row
        out[...] = jnp.sum(jnp.where(keep, found, 0.0), axis=0, keepdims=True)

    size = v[7].shape[0]
    index = me.owner * size + counter((1, size), 1)
    keeper = holder(index, hidden, cores)
    pick(hidden, size, keeper, index - keeper * hidden, 5, r.bu_out)
    size = 3 * own
    index = me.owner * size + counter((1, size), 1)
    part = holder(index, features, 3)
    index = index - part * features
    keeper = holder(index, width, cores)
    pick(3 * width, size, keeper, index - keeper * width + part * width, 6, r.bq_out)

    column_end(0, q_end)
    for n, whole in enumerate((r.gd_out, r.gp_out)):
        half = whole.shape[0] // 2
        net.arrived(whole.at[block(1 - c, half)], half_slot + n)
    assert net.used <= r.send.shape[0]
    net.finish()


def finish_kernel(output, grad_x, q_end, u_end, gp, gd, five, bq, bu, *finals):
    (
        output_f,
        grad_x_f,
        gain_a,
        shift_a,
        gq_f,
        bq_f,
        gp_f,
        bp_f,
        gain_m,
        shift_m,
        gu_f,
        bu_f,
        gd_f,
        bd_f,
    ) = finals
    output_f[...] = output[...]
    grad_x_f[...] = grad_x[...]
    cores, _, hidden = u_end.shape
    width = q_end.shape[2] // 3
    for b in range(cores):
        gu_f[:, b * hidden : (b + 1) * hidden] = u_end[b].astype(F32)
        for part in range(3):
            at = (part * cores + b) * width
            gq_f[:, at : at + width] = q_end[b, :, part * width : (part + 1) * width].astype(F32)
    gp_f[...] = gp[...]
    gd_f[...] = gd[...]
    for n, leaf in enumerate((gain_a, shift_a, gain_m, shift_m, bp_f)):
        leaf[...] = five[n]
    bd_f[...] = five[4]
    bq_f[...] = bq[0]
    bu_f[...] = bu[0]


def turn_tables(width, head_dim):
    half = ROT // 2
    frequency = THETA ** (-2.0 * np.arange(half) / ROT)
    angles = np.arange(SEQ)[:, None] * frequency[None, :]
    cosine, sine = np.cos(angles), np.sin(angles)
    rest = head_dim - ROT
    heads = width // head_dim
    one = np.ones((SEQ, rest))
    none = np.zeros((SEQ, rest))
    zero = np.zeros((SEQ, half))
    tables = (
        [cosine, cosine, one],
        [-sine, zero, none],
        [zero, sine, none],
    )
    return [np.concatenate(parts * heads, axis=1).astype(np.float32) for parts in tables]


def local(
    inputs,
    cotangent,
    attn_gain,
    attn_shift,
    qkv_weight,
    qkv_bias,
    proj_weight,
    proj_bias,
    mlp_gain,
    mlp_shift,
    up_weight,
    up_bias,
    down_weight,
    down_bias,
):
    owners = lax.axis_size("fsdp")
    replicas = lax.axis_size("replica")
    rows, features = inputs.shape
    line, plane = degrees(owners, features)
    cores = 2 * line
    count = cores * rows
    head_dim = features // H
    width, hidden = features // cores, up_weight.shape[1] // cores
    own = features // owners
    proj_rows, down_rows = proj_weight.shape[0], down_weight.shape[0]
    heads = width // head_dim
    reach = -(-max(v.shape[0] for v in (attn_gain, qkv_bias, up_bias)) // LANES) * LANES

    vectors = (attn_gain, attn_shift, mlp_gain, mlp_shift, proj_bias, down_bias, qkv_bias, up_bias)
    outs = dict(
        output=((rows, features), BF16),
        grad_x=((rows, features), BF16),
        q_end=((cores, own, 3 * width), BF16),
        u_end=((cores, own, hidden), BF16),
        gp_out=((proj_rows, features), F32),
        gd_out=((down_rows, features), F32),
        five_out=((8, own), F32),
        bq_out=((1, 3 * own), F32),
        bu_out=((1, up_bias.shape[0]), F32),
    )
    tables = turn_tables(width, head_dim)
    scratch = dict(
        x_all=((count, features), BF16),
        cot_all=((count, features), BF16),
        wq=((features, 3 * width), BF16),
        wp=((width, features), BF16),
        wu=((features, hidden), BF16),
        wd=((hidden, features), BF16),
        vec_own=((8, reach), F32),
        vec_all=((owners, 8, reach), F32),
        rows8=((8, features), F32),
        bias_q=((1, 3 * width), F32),
        bias_u=((1, hidden), F32),
        mean=((count, 1), F32),
        inverse=((count, 1), F32),
        attn_in=((count, features), BF16),
        attn_in_t=((features, count), BF16),
        mlp_in=((count, features), BF16),
        mlp_in_t=((features, count), BF16),
        q_s=((count, width), BF16),
        k_s=((count, width), BF16),
        v_s=((count, width), BF16),
        probs=((count // SEQ, heads, SEQ, SEQ), F32),
        ctx=((count, width), BF16),
        ctx_t=((width, count), BF16),
        act=((count, hidden), BF16),
        act_t=((hidden, count), BF16),
        slope=((count, hidden), F32),
        gpre=((count, hidden), BF16),
        gcol=((count, 3 * width), BF16),
        gctx=((count, width), BF16),
        out_part=((count, features), BF16),
        back_part=((count, features), BF16),
        gq=((line, plane, own, 3 * width), BF16),
        gp=((width, features), BF16),
        gu=((line, plane, own, hidden), BF16),
        gd=((hidden, features), BF16),
        rows_in=((2, line, rows, features), BF16),
        rows_mid=((2, line, rows, features), BF16),
        rows_end=((2, line, rows, features), BF16),
        relay_in=((2, 2, rows, features), BF16),
        total=((rows, features), F32),
        q_in=((plane, line, own, 3 * width), BF16),
        u_in=((plane, line, own, hidden), BF16),
        q_mid=((line, own, 3 * width), BF16),
        u_mid=((line, own, hidden), BF16),
        p_in=((plane, proj_rows // 2, features), BF16),
        d_in=((plane, down_rows // 2, features), BF16),
        sums=((8, features), F32),
        sums_in=((plane, 8, features), F32),
        sums_all=((cores, 8, features), F32),
    )
    scratch.update(zip(("v%d" % n for n in range(8)), ((v.shape, BF16) for v in vectors)))
    scratch.update(
        cosine=((SEQ, width), F32), back_sine=((SEQ, width), F32), fore_sine=((SEQ, width), F32)
    )
    operands = (inputs, cotangent, qkv_weight, proj_weight, up_weight, down_weight, *vectors, *tables)
    operands = [pltpu.with_memory_space_constraint(a, pltpu.HBM) for a in operands]
    sems = 20 + 18 * line + 10 * plane
    vmem = pl.BlockSpec(memory_space=pltpu.VMEM)
    results = pl.pallas_call(
        functools.partial(layer_kernel, line, plane, head_dim, list(outs) + list(scratch)),
        out_shape=[jax.ShapeDtypeStruct(*outs[name]) for name in outs],
        in_specs=[pl.BlockSpec(memory_space=pltpu.HBM)] * 17,
        out_specs=[vmem] * len(outs),
        scratch_shapes=[pltpu.VMEM(*scratch[name]) for name in scratch]
        + [pltpu.SemaphoreType.DMA((sems,)), pltpu.SemaphoreType.DMA((sems,))],
        compiler_params=pltpu.CompilerParams(
            collective_id=0, has_side_effects=True, vmem_limit_bytes=VMEM_BYTES
        ),
        name="layer",
    )(*operands)
    gradients = (
        ((own,), F32),
        ((own,), F32),
        ((own, 3 * features), F32),
        ((3 * own,), F32),
        ((proj_rows, features), F32),
        ((own,), F32),
        ((own,), F32),
        ((own,), F32),
        ((own, cores * hidden), F32),
        (up_bias.shape, F32),
        ((down_rows, features), F32),
        ((own,), F32),
    )
    final = tuple(outs.values())[:2] + gradients
    final = pl.pallas_call(
        finish_kernel,
        out_shape=[jax.ShapeDtypeStruct(*leaf) for leaf in final],
        in_specs=[vmem] * len(outs),
        out_specs=[vmem] * len(final),
        compiler_params=pltpu.CompilerParams(vmem_limit_bytes=VMEM_BYTES),
        name="finish",
    )(*results)
    final = list(final)
    if replicas > 2:
        groups = [[j for j in range(replicas) if j % 2 == k] for k in range(2)]
        final[2:] = lax.psum(tuple(final[2:]), "replica", axis_index_groups=groups)
    return tuple(final)


def solution(mesh):
    return jax.shard_map(
        local,
        mesh=mesh,
        in_specs=(
            P(("fsdp", "replica"), None),
            P(("fsdp", "replica"), None),
            P("fsdp"),
            P("fsdp"),
            P("fsdp", None),
            P("fsdp"),
            P("fsdp", None),
            P("fsdp"),
            P("fsdp"),
            P("fsdp"),
            P("fsdp", None),
            P("fsdp"),
            P("fsdp", None),
            P("fsdp"),
        ),
        out_specs=(
            P(("fsdp", "replica"), None),
            P(("fsdp", "replica"), None),
            P("fsdp"),
            P("fsdp"),
            P("fsdp", None),
            P("fsdp"),
            P("fsdp", None),
            P("fsdp"),
            P("fsdp"),
            P("fsdp"),
            P("fsdp", None),
            P("fsdp"),
            P("fsdp", None),
            P("fsdp"),
        ),
        check_vma=False,
    )
```

```python
import functools
import math

import jax
import jax.numpy as jnp
import numpy as np
from jax import lax
from jax.experimental import pallas as pl
from jax.experimental.pallas import tpu as pltpu
from jax.sharding import PartitionSpec as P

H = 16
ROT = 16
SEQ = 128


EPSILON = 1e-05
THETA = 10000.0
SQRT_HALF = 0.7071067811865476
INV_ROOT_TAU = 0.3989422804014327


MESH = pl.DeviceIdType.MESH
LANES = 128
BF16 = jnp.bfloat16
F32 = jnp.float32
VMEM_BYTES = 48 * 1024 * 1024


def degrees(owners, features):
    line = math.gcd(owners, features // (2 * LANES))
    return line, owners // line


class Place:
    def __init__(self, line, plane):
        self.line, self.plane = line, plane
        self.owner = lax.axis_index("fsdp")
        replica = lax.axis_index("replica")
        self.t = lax.div(self.owner, plane)
        self.i = lax.rem(self.owner, plane)
        self.c = lax.rem(replica, 2)
        self.base = replica - self.c

    def at(self, t, i, c):
        return (t * self.plane + i, self.base + c)

    def on_line(self, k):
        return lax.rem(self.t + (k + self.line), self.line)

    def in_plane(self, k):
        return lax.rem(self.i + (k + self.plane), self.plane)

    def ends(self, k):
        if self.line < 3 or k not in (1, self.line - 1):
            return None
        return self.t == (0 if k == self.line - 1 else self.line - 1)

    def comes_far(self, k):
        if self.line < 3 or k not in (1, self.line - 1):
            return None
        return self.t == (self.line - 1 if k == self.line - 1 else 0)

    def greet(self):
        barrier = pltpu.get_barrier_semaphore()
        peers = [self.at(self.on_line(k), self.i, self.c) for k in range(1, self.line)]
        peers += [self.at(self.t, self.in_plane(k), self.c) for k in range(1, self.plane)]
        peers += [self.at(self.t, self.in_plane(k), 1 - self.c) for k in range(self.plane)]
        for peer in peers:
            pl.semaphore_signal(barrier, inc=1, device_id=peer, device_id_type=MESH)
        pl.semaphore_wait(barrier, len(peers))


class Copies:
    def __init__(self, send, recv):
        self.send, self.recv = send, recv
        self.used = 0
        self.last = []

    def slots(self, count):
        first = self.used
        self.used += count
        return first

    def push(self, src, dst, peer, slot, land=None):
        pltpu.make_async_remote_copy(
            src_ref=src,
            dst_ref=dst,
            send_sem=self.send.at[slot],
            recv_sem=self.recv.at[slot if land is None else land],
            device_id=peer,
            device_id_type=MESH,
        ).start()

    def local(self, src, dst, slot):
        pltpu.make_async_copy(src, dst, self.recv.at[slot]).start()

    def arrived(self, ref, slot):
        pltpu.make_async_copy(ref, ref, self.recv.at[slot]).wait()

    def left(self, ref, slot):
        pltpu.make_async_copy(ref, ref, self.send.at[slot]).wait()

    def later(self, ref, slots, when=None):
        def done():
            for slot in slots:
                self.left(ref, slot)

        self.last.append(done if when is None else lambda: pl.when(when)(done))

    def finish(self):
        for done in self.last:
            done()


def block(index, size):
    return pl.ds(pl.multiple_of(index * size, size), size)


def dot(left, right):
    return jnp.dot(left, right, preferred_element_type=F32)


def dot_last(left, right):
    return lax.dot_general(left, right, (((1,), (1,)), ((), ())), preferred_element_type=F32)


def exact_dot(left, right):
    return jnp.dot(left, right, preferred_element_type=F32, precision=lax.Precision.HIGHEST)


def counter(dims, axis):
    return lax.broadcasted_iota(jnp.int32, dims, axis)


def holder(index, width, count):
    found = jnp.zeros_like(index)
    for k in range(1, count):
        found = found + (index >= k * width).astype(jnp.int32)
    return found


class Refs:
    def __init__(self, refs, named):
        self.x, self.cot, self.wqkv, self.wproj, self.wup, self.wdown = refs[:6]
        self.small = refs[6:17]
        self.send, self.recv = refs[-2:]
        self.__dict__.update(zip(named, refs[17:-2]))


def layer_kernel(line, plane, head_dim, named, *refs):
    r = Refs(refs, named)
    me = Place(line, plane)
    t, i, c = me.t, me.i, me.c
    net = Copies(r.send, r.recv)
    owners, cores, group = line * plane, 2 * line, plane // 2
    x, cot, wqkv, wup = r.x, r.cot, r.wqkv, r.wup
    x_all, cot_all, wq, wp, wu, wd = r.x_all, r.cot_all, r.wq, r.wp, r.wu, r.wd
    rows, features = x.shape
    count = cores * rows
    pair = 2 * rows
    width = features // cores
    hidden = wup.shape[1] // cores
    own = features // owners
    span = features // line
    heads = width // head_dim
    piece = 2 * t + c
    mine = block(piece, rows)
    partner = me.at(t, i, 1 - c)
    small = [r.v0, r.v1, r.v2, r.v3, r.v4, r.v5, r.v6, r.v7, r.cosine, r.back_sine, r.fore_sine]
    v = small[:8]
    vec_own, vec_all = r.vec_own, r.vec_all
    reach = vec_own.shape[1]

    relays, adders = [], []
    if line > 2:
        adders = [(line - 2, 1), (2 % line, line - 2)]
        relays = [(line - 2, line - 2, 1, line - 1), (2 % line, 1, -1, 1)]
    relay_first = sorted({at_k for at_k, *_ in relays})
    relay_last = [k for k in range(1, line) if k not in relay_first]

    small_slot = net.slots(len(small))
    for n, ref in enumerate(small):
        net.local(r.small[n], ref, small_slot + n)
    me.greet()
    for n, ref in enumerate(small):
        net.arrived(ref, small_slot + n)

    vec_own[...] = jnp.zeros_like(vec_own)
    for n in range(8):
        size = v[n].shape[0]
        vec_own[n : n + 1, :size] = v[n][...].astype(F32).reshape(1, size)
    vec_all[me.owner] = vec_own[...]
    vec_first = net.slots(1)
    for k in range(1, plane):
        net.push(vec_own, vec_all.at[me.owner], me.at(t, me.in_plane(k), c), vec_first)
    net.later(vec_all.at[: plane - 1], [vec_first])

    col_slot = net.slots(2 * line)
    shard = pl.ds(pl.multiple_of(t * span + i * own, own), own)
    def move(k, n, src, dst):
        slot = col_slot + 2 * k + n
        if k == 0:
            net.local(src, dst, slot)
        else:
            net.push(src, dst, me.at(me.on_line(k), i, c), slot)

    for k in range(line):
        for part in range(3):
            at = (part * cores + 2 * me.on_line(k) + c) * width
            src = wqkv.at[:, pl.ds(pl.multiple_of(at, LANES), width)]
            move(k, 0, src, wq.at[shard, part * width : (part + 1) * width])

    def send_tokens(src, whole):
        line_slot = net.slots(line)
        pair_slot = net.slots(line)
        pass_slot = net.slots(2)
        for k in relay_first + relay_last:
            far = me.ends(k)
            near = None if far is None else jnp.logical_not(far)
            send = lambda: net.push(
                src, whole.at[mine], me.at(me.on_line(k), i, c), line_slot + k
            )
            net.later(whole.at[mine], [line_slot + k], near)
            for _, at_t, _, land in relays if line > 3 else []:
                if k == land:
                    ready = t != at_t
                    near = ready if near is None else jnp.logical_and(near, ready)
            send() if near is None else pl.when(near)(send)
        net.local(src, whole.at[mine], line_slot)
        net.push(src, whole.at[mine], partner, pair_slot)
        net.later(whole.at[mine], range(pair_slot, pair_slot + line))
        return line_slot, pair_slot, pass_slot, src

    def pass_tokens(whole, slots, distances):
        line_slot, pair_slot, pass_slot, src = slots
        for k in distances:
            ref = whole.at[block(2 * me.on_line(-k) + c, rows)]
            net.arrived(ref, line_slot + k)
            for n, (at_k, at_t, step, land) in enumerate(relays):
                if k == at_k:

                    @pl.when(t == at_t)
                    def _():
                        peer = me.at(me.on_line(step), i, c)
                        net.push(ref, ref, peer, pass_slot + n, line_slot + land)
                        if line > 3:
                            peer = me.at(me.on_line(-step), i, c)
                            net.push(src, whole.at[mine], peer, line_slot + land)

                    net.later(ref, [pass_slot + n], t == at_t)
            net.push(ref, ref, partner, pair_slot + k)

    def other_tokens(whole, slots):
        for k in range(line):
            net.arrived(whole.at[block(2 * me.on_line(-k) + 1 - c, rows)], slots[1] + k)
        net.arrived(whole.at[mine], slots[0])

    x_slots = send_tokens(x, x_all)
    for k in range(line):
        move(k, 1, wup.at[:, block(2 * me.on_line(k) + c, hidden)], wu.at[shard])

    def rows_out(source, whole):
        height = source.shape[0]
        half = height // 2
        core = lax.div(i, group)
        src = source.at[block(c, half)]
        dst = whole.at[
            pl.ds(pl.multiple_of(lax.rem(i, group) * height + c * half, half), half)
        ]
        first = net.slots(2 * plane)
        away = net.slots(plane)
        for k in range(1, plane):
            net.push(src, dst, me.at(t, me.in_plane(k), core), away + k, first + 2 * k + c)
        net.later(dst, range(away + 1, away + plane))

        @pl.when(core == c)
        def _():
            net.local(src, dst, first + c)

        @pl.when(core != c)
        def _():
            net.push(src, dst, me.at(t, i, core), away, first + c)

        net.last.append(lambda: pl.when(core != c)(lambda: net.left(dst, away)))

        def wait():
            for k in range(plane):
                origin = me.in_plane(-k)

                @pl.when(lax.div(origin, group) == c)
                def _():
                    for s in range(2):
                        at = lax.rem(origin, group) * height + s * half
                        net.arrived(
                            whole.at[pl.ds(pl.multiple_of(at, half), half)], first + 2 * k + s
                        )

        return wait


    onward = net.slots(2)

    def strip(source, owner):
        return pl.ds(pl.multiple_of(source * span + owner * own, own), own)

    net.arrived(vec_all.at[: plane - 1], vec_first)
    vec_second = net.slots(1)
    bundle = vec_all.at[pl.ds(t * plane, plane)]
    for k in range(1, line):
        net.push(bundle, bundle, me.at(me.on_line(k), i, c), vec_second)
    others = vec_all.at[: (line - 1) * plane]
    if line > 1:
        net.later(others, [vec_second])

    def columns_on(whole, n):
        for k in range(line):
            at = strip(me.on_line(-k), i)
            net.arrived(whole.at[at], col_slot + 2 * k + n)
            if k > 0:
                net.later(whole.at[at], [col_slot + 2 * k + n])
            for j in range(1, plane):
                net.push(whole.at[at], whole.at[at], me.at(t, me.in_plane(j), c), onward + n)
        net.later(whole.at[: line * (plane - 1) * own], [onward + n])

    columns_on(wq, 0)
    wp_wait = rows_out(r.wproj, wp)
    wd_wait = rows_out(r.wdown, wd)
    columns_on(wu, 1)

    def wait_columns(whole, n):
        net.arrived(whole.at[: line * (plane - 1) * own], onward + n)

    pass_tokens(x_all, x_slots, relay_first + relay_last)
    cot_slots = send_tokens(cot, cot_all)

    if line > 1:
        net.arrived(others, vec_second)
    flat = vec_all[...].reshape(owners * 8, reach).astype(BF16)

    def unpack(index, size):
        keeper = holder(index, size, owners)
        spread = (counter((size, index.shape[1]), 0) == index - keeper * size).astype(BF16)
        return dot(flat[:, :size], spread), keeper

    index = counter((1, features), 1)
    spread, keeper = unpack(index, own)
    spread = spread.reshape(owners, 8, features)
    keep = counter((owners, 8, features), 0) == keeper.reshape(1, 1, features)
    r.rows8[...] = jnp.sum(jnp.where(keep, spread, 0.0), axis=0)

    index = counter((1, 3 * width), 1)
    part = holder(index, width, 3)
    index = index + part * (features - width) + piece * width
    spread, keeper = unpack(index, 3 * own)
    keep = counter((owners * 8, 3 * width), 0) == keeper * 8 + 6
    r.bias_q[...] = jnp.sum(jnp.where(keep, spread, 0.0), axis=0, keepdims=True)
    index = counter((1, hidden), 1) + piece * hidden
    spread, keeper = unpack(index, v[7].shape[0])
    keep = counter((owners * 8, hidden), 0) == keeper * 8 + 7
    r.bias_u[...] = jnp.sum(jnp.where(keep, spread, 0.0), axis=0, keepdims=True)
    g_attn, b_attn, g_mlp, b_mlp = (r.rows8[n : n + 1, :] for n in range(4))

    attn_in, mlp_in = r.attn_in, r.mlp_in
    other_tokens(x_all, x_slots)

    def norm_step(j, carry):
        at = block(j, rows)
        data = x_all[at].astype(F32)
        mean = jnp.mean(data, axis=-1, keepdims=True)
        centered = data - mean
        inverse = lax.rsqrt(jnp.mean(centered * centered, axis=-1, keepdims=True) + EPSILON)
        r.mean[at] = mean
        r.inverse[at] = inverse
        unit = centered * inverse
        a = (unit * g_attn + b_attn).astype(BF16)
        m = (unit * g_mlp + b_mlp).astype(BF16)
        attn_in[at] = a
        mlp_in[at] = m
        r.attn_in_t[:, at] = a.T
        r.mlp_in_t[:, at] = m.T
        return carry

    lax.fori_loop(0, cores, norm_step, 0)

    half_rot = ROT // 2

    def turn(data, sign):
        seqs = data.shape[0] // SEQ
        cosine, back_sine, fore_sine = (
            jnp.concatenate([table[...]] * seqs, axis=0) if seqs > 1 else table[...]
            for table in (r.cosine, r.back_sine, r.fore_sine)
        )
        moved = (
            pltpu.roll(data, data.shape[1] - half_rot, 1) * back_sine
            + pltpu.roll(data, half_rot, 1) * fore_sine
        )
        return data * cosine + (moved if sign > 0 else -moved)

    wait_columns(wq, 0)

    def project_step(j, carry):
        at = block(j, pair)
        projected = dot(attn_in[at], wq[...]) + r.bias_q[...]
        r.q_s[at] = turn(projected[:, :width], 1).astype(BF16)
        r.k_s[at] = turn(projected[:, width : 2 * width], 1).astype(BF16)
        r.v_s[at] = projected[:, 2 * width :].astype(BF16)
        return carry

    lax.fori_loop(0, line, project_step, 0)

    lane = counter((SEQ, width), 1)

    def of_head(data, h):
        inside = (lane >= h * head_dim) & (lane < (h + 1) * head_dim)
        return jnp.where(inside, data, jnp.zeros_like(data))

    scale = head_dim ** (-0.5)

    def attend_step(s, carry):
        at = block(s, SEQ)
        queries, keys_rot, values = r.q_s[at], r.k_s[at], r.v_s[at]
        causal = counter((SEQ, SEQ), 0) >= counter((SEQ, SEQ), 1)
        total = jnp.zeros((SEQ, width), F32)
        for h in range(heads):
            scores = dot_last(of_head(queries, h), keys_rot) * scale
            scores = jnp.where(causal, scores, -jnp.inf)
            peak = jnp.max(scores, axis=-1, keepdims=True)
            logsum = peak + jnp.log(jnp.sum(jnp.exp(scores - peak), axis=-1, keepdims=True))
            probs = jnp.exp(scores - logsum)
            r.probs[s, h] = probs
            total = total + dot(probs.astype(BF16), of_head(values, h))
        context = total.astype(BF16)
        r.ctx[at] = context
        r.ctx_t[:, at] = context.T
        return carry

    lax.fori_loop(0, count // SEQ, attend_step, 0)

    pass_tokens(cot_all, cot_slots, relay_first)
    wait_columns(wu, 1)

    def hidden_step(j, carry):
        at = block(j, pair)
        pre = dot(mlp_in[at], wu[...]) + r.bias_u[...]
        chance = 0.5 * (1.0 + lax.erf(pre * SQRT_HALF))
        act = (pre * chance).astype(BF16)
        r.slope[at] = chance + pre * jnp.exp(-0.5 * pre * pre) * INV_ROOT_TAU
        r.act[at] = act
        r.act_t[:, at] = act.T
        return carry

    lax.fori_loop(0, line, hidden_step, 0)
    wp_wait()
    wd_wait()

    rows_in, rows_mid, rows_end = r.rows_in, r.rows_mid, r.rows_end
    swap_slot = net.slots(2 * line)
    end_slot = net.slots(2 * line)

    def swap(n, part, j):
        net.push(
            part.at[block(2 * j + 1 - c, rows)], rows_in.at[n, j], partner, swap_slot + n * line + j
        )

    relay_slot = net.slots(4)
    relay_in = r.relay_in
    end = (t == 0) | (t == line - 1) if line > 2 else None

    def send_sum(n, k):
        slot = end_slot + n * line + k
        to = me.on_line(k)
        net.push(rows_mid.at[n, to], rows_end.at[n, k], me.at(to, i, c), slot)

    def add_up(n, part):
        for k in [line - 1] + list(range(1, line - 1)) + [line] if line > 1 else [line]:
            to = me.on_line(k)
            net.arrived(rows_in.at[n, to], swap_slot + n * line + to)
            both = part[block(2 * to + c, rows)].astype(F32) + rows_in[n, to].astype(F32)
            rows_mid[n, to] = both.astype(BF16)
            if k == line:
                continue
            direct = jnp.bool_(True)
            far = me.ends(k)
            if far is not None:
                way = 0 if k == line - 1 else 1

                @pl.when(far)
                def _():
                    peer = me.at(line - 2 if k == 1 else 1, i, c)
                    slot = relay_slot + 2 * n + way
                    net.push(rows_mid.at[n, to], relay_in.at[n, way], peer, slot)

                direct = jnp.logical_not(far)
            net.later(rows_mid.at[n, to], [end_slot + n * line + k], direct)
            for at_k, at_t in adders:
                if k == at_k:
                    direct = jnp.logical_and(direct, t != at_t)
            pl.when(direct if end is None else jnp.logical_and(direct, jnp.logical_not(end)))(
                lambda: send_sum(n, k)
            )
        net.later(rows_in.at[n, 0], range(swap_slot + n * line, swap_slot + (n + 1) * line))

    def add_rest(n):
        if end is None:
            return

        @pl.when(end)
        def _():
            for way, last in enumerate((0, line - 1)):

                @pl.when(t == last)
                def _():
                    net.left(rows_mid.at[n, 0], relay_slot + 2 * n + way)

            for k in [2 % line] + [1, line - 1]:
                if k == 2 % line and k in (1, line - 1):
                    continue
                far = me.ends(k)
                send = lambda: send_sum(n, k)
                send() if far is None else pl.when(jnp.logical_not(far))(send)
            for k in range(3, line - 1):
                send_sum(n, k)

    def relay_up(n):
        for way, (k, at_t) in enumerate(adders):

            @pl.when(t == at_t)
            def _():
                to = me.on_line(k)
                net.arrived(relay_in.at[n, way], relay_slot + 2 * n + way)
                both = rows_mid[n, to].astype(F32) + relay_in[n, way].astype(F32)
                rows_mid[n, to] = both.astype(BF16)
                send_sum(n, k)

    def row_total(n):
        total = r.total
        total[...] = rows_mid[n, t].astype(F32)
        for k in range(1, line):

            def more():
                net.arrived(rows_end.at[n, k], end_slot + n * line + k)
                total[...] += rows_end[n, k].astype(F32)

            far = me.comes_far(k)
            more() if far is None else pl.when(jnp.logical_not(far))(more)
        return total[...]

    def out_step(j, carry):
        at = block(j, pair)
        part = dot(r.ctx[at], wp[...]) + dot(r.act[at], wd[...])
        r.out_part[at] = part.astype(BF16)
        swap(0, r.out_part, j)
        return carry

    lax.fori_loop(0, line, out_step, 0)
    add_up(0, r.out_part)

    pass_tokens(cot_all, cot_slots, relay_last)
    other_tokens(cot_all, cot_slots)

    def rows_back(source, landing):
        height = source.shape[0] // group
        half = height // 2
        slot = net.slots(2 * plane)
        for k in range(plane):
            to = me.in_plane(k)

            @pl.when(lax.div(to, group) == c)
            def _():
                for s in range(2):
                    src = source.at[
                        pl.ds(pl.multiple_of(lax.rem(to, group) * height + s * half, half), half)
                    ]
                    send = lambda: net.push(
                        src, landing.at[k], me.at(t, to, s), slot + 2 * k + s, slot + k
                    )
                    if k == 0:
                        pl.when(c == s)(lambda: net.local(src, landing.at[k], slot + k))
                        pl.when(c != s)(send)
                    else:
                        send()

        def arrive():
            for k in range(plane):
                net.arrived(landing.at[k], slot + k)

        def leave():
            for k in range(plane):
                to = me.in_plane(k)

                @pl.when(lax.div(to, group) == c)
                def _():
                    for s in range(2):
                        done = lambda: net.left(landing.at[k], slot + 2 * k + s)
                        if k == 0:
                            pl.when(c != s)(done)
                        else:
                            done()

        net.last.append(leave)
        return arrive

    def down_step(j, carry):
        at = block(j, LANES)
        r.gd[at] = dot(r.act_t[at], cot_all[...]).astype(BF16)
        return carry

    lax.fori_loop(0, hidden // LANES, down_step, 0)
    d_arrive = rows_back(r.gd, r.d_in)
    add_rest(0)
    relay_up(0)

    sums = r.sums
    sums[...] = jnp.zeros_like(sums)

    def slope_step(j, carry):
        at = block(j, pair)
        grad = dot_last(cot_all[at], wd[...]) * r.slope[at]
        sums[5:6, :hidden] += jnp.sum(grad, axis=0, keepdims=True)
        r.gpre[at] = grad.astype(BF16)
        r.gctx[at] = dot_last(cot_all[at], wp[...]).astype(BF16)
        return carry

    lax.fori_loop(0, line, slope_step, 0)

    q_in, u_in = r.q_in, r.u_in
    col_back = net.slots(2)

    def up_step(j, carry):
        grad = dot(r.mlp_in_t[block(j, span)], r.gpre[...]).astype(BF16)
        r.gu[j] = grad.reshape(plane, own, hidden)
        return carry

    lax.fori_loop(0, line, up_step, 0)
    for k in range(1, plane):
        to = me.in_plane(k)
        net.push(r.gu.at[:, to], u_in.at[k], me.at(t, to, c), col_back + 1)
    net.later(u_in.at[: plane - 1], [col_back + 1])

    def attend_back_step(s, carry):
        at = block(s, SEQ)
        queries, keys_rot, values, upper = r.q_s[at], r.k_s[at], r.v_s[at], r.gctx[at]
        g_queries = jnp.zeros((SEQ, width), F32)
        g_keys = jnp.zeros((SEQ, width), F32)
        g_values = jnp.zeros((SEQ, width), F32)
        for h in range(heads):
            probs = r.probs[s, h]
            upper_h = of_head(upper, h)
            g_probs = dot_last(upper_h, values)
            g_values = g_values + dot(probs.astype(BF16).T, upper_h)
            g_scores = (
                probs * (g_probs - jnp.sum(probs * g_probs, axis=-1, keepdims=True)) * scale
            ).astype(BF16)
            g_queries = g_queries + dot(g_scores, of_head(keys_rot, h))
            g_keys = g_keys + dot(g_scores.T, of_head(queries, h))
        parts = (turn(g_queries, -1), turn(g_keys, -1), g_values)
        for n, grad in enumerate(parts):
            lanes = slice(n * width, (n + 1) * width)
            sums[6:7, lanes] += jnp.sum(grad, axis=0, keepdims=True)
            r.gcol[at, lanes] = grad.astype(BF16)
        return carry

    lax.fori_loop(0, count // SEQ, attend_back_step, 0)

    def back_step(j, carry):
        at = block(j, pair)
        unit = (x_all[at].astype(F32) - r.mean[at]) * r.inverse[at]
        g_a = dot_last(r.gcol[at], wq[...])
        sums[0:1, :] += jnp.sum(g_a * unit, axis=0, keepdims=True)
        sums[1:2, :] += jnp.sum(g_a, axis=0, keepdims=True)
        g_m = dot_last(r.gpre[at], wu[...])
        sums[2:3, :] += jnp.sum(g_m * unit, axis=0, keepdims=True)
        sums[3:4, :] += jnp.sum(g_m, axis=0, keepdims=True)
        part = g_a * r.rows8[0:1, :] + g_m * r.rows8[2:3, :]
        r.back_part[at] = part.astype(BF16)
        swap(1, r.back_part, j)
        return carry

    lax.fori_loop(0, line, back_step, 0)
    add_up(1, r.back_part)
    sums[4:5, :] = jnp.sum(cot_all[mine].astype(F32), axis=0, keepdims=True)

    def qkv_step(j, carry):
        grad = dot(r.attn_in_t[block(j, span)], r.gcol[...]).astype(BF16)
        r.gq[j] = grad.reshape(plane, own, 3 * width)
        return carry

    lax.fori_loop(0, line, qkv_step, 0)
    for k in range(1, plane):
        to = me.in_plane(k)
        net.push(r.gq.at[:, to], q_in.at[k], me.at(t, to, c), col_back)
    net.later(q_in.at[: plane - 1], [col_back])
    add_rest(1)
    relay_up(1)
    r.gp[...] = dot(r.ctx_t[...], cot_all[...]).astype(BF16)
    p_arrive = rows_back(r.gp, r.p_in)

    sums_in, sums_all = r.sums_in, r.sums_all
    sum_slot = net.slots(1)
    for k in range(1, plane):
        net.push(sums, sums_in.at[k], me.at(t, me.in_plane(k), c), sum_slot)
    net.later(sums_in.at[: plane - 1], [sum_slot])

    q_mid, u_mid, q_end, u_end = r.q_mid, r.u_mid, r.q_end, r.u_end
    third = net.slots(2 * line)
    fourth = net.slots(2 * line)

    def column_total(n, source, landing, middle, end):
        net.arrived(landing.at[: plane - 1], col_back + n)
        for b in range(line):
            total = source[b, i].astype(F32)
            for k in range(1, plane):
                total = total + landing[k, b].astype(F32)
            middle[b] = total.astype(BF16)
        for k in range(1, line):
            to = me.on_line(k)
            net.push(middle.at[to], end.at[piece], me.at(to, i, c), third + 2 * k + n)
            net.later(middle.at[to], [third + 2 * k + n])
        end[piece] = middle[t]
        net.push(end.at[piece], end.at[piece], partner, fourth + n)
        net.later(end.at[piece], [fourth + 2 * k + n for k in range(line)])

    def column_pass(n, end):
        for k in range(1, line):
            ref = end.at[2 * me.on_line(-k) + c]
            net.arrived(ref, third + 2 * k + n)
            net.push(ref, ref, partner, fourth + 2 * k + n)

    def column_end(n, end):
        for k in range(line):
            net.arrived(end.at[2 * me.on_line(-k) + 1 - c], fourth + 2 * k + n)

    column_total(1, r.gu, u_in, u_mid, u_end)

    half_slot = net.slots(2)

    def row_end(n, landing, whole, arrive):
        arrive()
        half = landing.shape[1]
        total = landing[0].astype(F32)
        for k in range(1, plane):
            total = total + landing[k].astype(F32)
        at = whole.at[block(c, half)]
        at[...] = total
        net.push(at, at, partner, half_slot + n)
        net.later(at, [half_slot + n])

    row_end(0, r.d_in, r.gd_out, d_arrive)

    net.arrived(sums_in.at[: plane - 1], sum_slot)
    total = sums[...]
    for k in range(1, plane):
        total = total + sums_in[k]
    sums_all[piece] = total
    sum_second = net.slots(line)
    sum_third = net.slots(line)
    ref = sums_all.at[piece]
    for k in range(1, line):
        net.push(ref, ref, me.at(me.on_line(k), i, c), sum_second + k)
    net.push(ref, ref, partner, sum_third)
    net.later(ref, range(sum_second + 1, sum_second + line))
    net.later(ref, range(sum_third, sum_third + line))

    column_total(0, r.gq, q_in, q_mid, q_end)
    row_end(1, r.p_in, r.gp_out, p_arrive)

    for k in range(1, line):
        ref = sums_all.at[2 * me.on_line(-k) + c]
        net.arrived(ref, sum_second + k)
        net.push(ref, ref, partner, sum_third + k)
    column_pass(1, u_end)

    data = x_all[mine].astype(F32)
    bias = r.rows8[4:5, :] + r.rows8[5:6, :]
    r.output[...] = (data + row_total(0) + bias).astype(BF16)
    unit = (data - r.mean[mine]) * r.inverse[mine]
    grad = row_total(1)
    grad = r.inverse[mine] * (
        grad
        - jnp.mean(grad, axis=-1, keepdims=True)
        - unit * jnp.mean(grad * unit, axis=-1, keepdims=True)
    )
    r.grad_x[...] = (cot_all[mine].astype(F32) + grad).astype(BF16)

    column_pass(0, q_end)
    column_end(1, u_end)

    for k in range(line):
        net.arrived(sums_all.at[2 * me.on_line(-k) + 1 - c], sum_third + k)
    every = sums_all[...]
    total = every[0]
    for b in range(1, cores):
        total = total + every[b]
    chosen = counter((features, own), 0) == me.owner * own + counter((features, own), 1)
    r.five_out[...] = exact_dot(total, chosen.astype(F32))
    stacked = every.reshape(cores * 8, features)

    def pick(columns, size, keeper, column, row, out):
        chosen = (counter((columns, size), 0) == column).astype(F32)
        found = exact_dot(stacked[:, :columns], chosen)
        keep = counter((cores * 8, size), 0) == keeper * 8 + row
        out[...] = jnp.sum(jnp.where(keep, found, 0.0), axis=0, keepdims=True)

    size = v[7].shape[0]
    index = me.owner * size + counter((1, size), 1)
    keeper = holder(index, hidden, cores)
    pick(hidden, size, keeper, index - keeper * hidden, 5, r.bu_out)
    size = 3 * own
    index = me.owner * size + counter((1, size), 1)
    part = holder(index, features, 3)
    index = index - part * features
    keeper = holder(index, width, cores)
    pick(3 * width, size, keeper, index - keeper * width + part * width, 6, r.bq_out)

    column_end(0, q_end)
    for n, whole in enumerate((r.gd_out, r.gp_out)):
        half = whole.shape[0] // 2
        net.arrived(whole.at[block(1 - c, half)], half_slot + n)
    assert net.used <= r.send.shape[0]
    net.finish()


def finish_kernel(output, grad_x, q_end, u_end, gp, gd, five, bq, bu, *finals):
    (
        output_f,
        grad_x_f,
        gain_a,
        shift_a,
        gq_f,
        bq_f,
        gp_f,
        bp_f,
        gain_m,
        shift_m,
        gu_f,
        bu_f,
        gd_f,
        bd_f,
    ) = finals
    output_f[...] = output[...]
    grad_x_f[...] = grad_x[...]
    cores, _, hidden = u_end.shape
    width = q_end.shape[2] // 3
    for b in range(cores):
        gu_f[:, b * hidden : (b + 1) * hidden] = u_end[b].astype(F32)
        for part in range(3):
            at = (part * cores + b) * width
            gq_f[:, at : at + width] = q_end[b, :, part * width : (part + 1) * width].astype(F32)
    gp_f[...] = gp[...]
    gd_f[...] = gd[...]
    for n, leaf in enumerate((gain_a, shift_a, gain_m, shift_m, bp_f)):
        leaf[...] = five[n]
    bd_f[...] = five[4]
    bq_f[...] = bq[0]
    bu_f[...] = bu[0]


def turn_tables(width, head_dim):
    half = ROT // 2
    frequency = THETA ** (-2.0 * np.arange(half) / ROT)
    angles = np.arange(SEQ)[:, None] * frequency[None, :]
    cosine, sine = np.cos(angles), np.sin(angles)
    rest = head_dim - ROT
    heads = width // head_dim
    one = np.ones((SEQ, rest))
    none = np.zeros((SEQ, rest))
    zero = np.zeros((SEQ, half))
    tables = (
        [cosine, cosine, one],
        [-sine, zero, none],
        [zero, sine, none],
    )
    return [np.concatenate(parts * heads, axis=1).astype(np.float32) for parts in tables]


def local(
    inputs,
    cotangent,
    attn_gain,
    attn_shift,
    qkv_weight,
    qkv_bias,
    proj_weight,
    proj_bias,
    mlp_gain,
    mlp_shift,
    up_weight,
    up_bias,
    down_weight,
    down_bias,
):
    owners = lax.axis_size("fsdp")
    replicas = lax.axis_size("replica")
    rows, features = inputs.shape
    line, plane = degrees(owners, features)
    cores = 2 * line
    count = cores * rows
    head_dim = features // H
    width, hidden = features // cores, up_weight.shape[1] // cores
    own = features // owners
    proj_rows, down_rows = proj_weight.shape[0], down_weight.shape[0]
    heads = width // head_dim
    reach = -(-max(v.shape[0] for v in (attn_gain, qkv_bias, up_bias)) // LANES) * LANES

    vectors = (attn_gain, attn_shift, mlp_gain, mlp_shift, proj_bias, down_bias, qkv_bias, up_bias)
    outs = dict(
        output=((rows, features), BF16),
        grad_x=((rows, features), BF16),
        q_end=((cores, own, 3 * width), BF16),
        u_end=((cores, own, hidden), BF16),
        gp_out=((proj_rows, features), F32),
        gd_out=((down_rows, features), F32),
        five_out=((8, own), F32),
        bq_out=((1, 3 * own), F32),
        bu_out=((1, up_bias.shape[0]), F32),
    )
    tables = turn_tables(width, head_dim)
    scratch = dict(
        x_all=((count, features), BF16),
        cot_all=((count, features), BF16),
        wq=((features, 3 * width), BF16),
        wp=((width, features), BF16),
        wu=((features, hidden), BF16),
        wd=((hidden, features), BF16),
        vec_own=((8, reach), F32),
        vec_all=((owners, 8, reach), F32),
        rows8=((8, features), F32),
        bias_q=((1, 3 * width), F32),
        bias_u=((1, hidden), F32),
        mean=((count, 1), F32),
        inverse=((count, 1), F32),
        attn_in=((count, features), BF16),
        attn_in_t=((features, count), BF16),
        mlp_in=((count, features), BF16),
        mlp_in_t=((features, count), BF16),
        q_s=((count, width), BF16),
        k_s=((count, width), BF16),
        v_s=((count, width), BF16),
        probs=((count // SEQ, heads, SEQ, SEQ), F32),
        ctx=((count, width), BF16),
        ctx_t=((width, count), BF16),
        act=((count, hidden), BF16),
        act_t=((hidden, count), BF16),
        slope=((count, hidden), F32),
        gpre=((count, hidden), BF16),
        gcol=((count, 3 * width), BF16),
        gctx=((count, width), BF16),
        out_part=((count, features), BF16),
        back_part=((count, features), BF16),
        gq=((line, plane, own, 3 * width), BF16),
        gp=((width, features), BF16),
        gu=((line, plane, own, hidden), BF16),
        gd=((hidden, features), BF16),
        rows_in=((2, line, rows, features), BF16),
        rows_mid=((2, line, rows, features), BF16),
        rows_end=((2, line, rows, features), BF16),
        relay_in=((2, 2, rows, features), BF16),
        total=((rows, features), F32),
        q_in=((plane, line, own, 3 * width), BF16),
        u_in=((plane, line, own, hidden), BF16),
        q_mid=((line, own, 3 * width), BF16),
        u_mid=((line, own, hidden), BF16),
        p_in=((plane, proj_rows // 2, features), BF16),
        d_in=((plane, down_rows // 2, features), BF16),
        sums=((8, features), F32),
        sums_in=((plane, 8, features), F32),
        sums_all=((cores, 8, features), F32),
    )
    scratch.update(zip(("v%d" % n for n in range(8)), ((v.shape, BF16) for v in vectors)))
    scratch.update(
        cosine=((SEQ, width), F32), back_sine=((SEQ, width), F32), fore_sine=((SEQ, width), F32)
    )
    operands = (inputs, cotangent, qkv_weight, proj_weight, up_weight, down_weight, *vectors, *tables)
    operands = [pltpu.with_memory_space_constraint(a, pltpu.HBM) for a in operands]
    sems = 20 + 18 * line + 10 * plane
    vmem = pl.BlockSpec(memory_space=pltpu.VMEM)
    results = pl.pallas_call(
        functools.partial(layer_kernel, line, plane, head_dim, list(outs) + list(scratch)),
        out_shape=[jax.ShapeDtypeStruct(*outs[name]) for name in outs],
        in_specs=[pl.BlockSpec(memory_space=pltpu.HBM)] * 17,
        out_specs=[vmem] * len(outs),
        scratch_shapes=[pltpu.VMEM(*scratch[name]) for name in scratch]
        + [pltpu.SemaphoreType.DMA((sems,)), pltpu.SemaphoreType.DMA((sems,))],
        compiler_params=pltpu.CompilerParams(
            collective_id=0, has_side_effects=True, vmem_limit_bytes=VMEM_BYTES
        ),
        name="layer",
    )(*operands)
    gradients = (
        ((own,), F32),
        ((own,), F32),
        ((own, 3 * features), F32),
        ((3 * own,), F32),
        ((proj_rows, features), F32),
        ((own,), F32),
        ((own,), F32),
        ((own,), F32),
        ((own, cores * hidden), F32),
        (up_bias.shape, F32),
        ((down_rows, features), F32),
        ((own,), F32),
    )
    final = tuple(outs.values())[:2] + gradients
    final = pl.pallas_call(
        finish_kernel,
        out_shape=[jax.ShapeDtypeStruct(*leaf) for leaf in final],
        in_specs=[vmem] * len(outs),
        out_specs=[vmem] * len(final),
        compiler_params=pltpu.CompilerParams(vmem_limit_bytes=VMEM_BYTES),
        name="finish",
    )(*results)
    final = list(final)
    if replicas > 2:
        groups = [[j for j in range(replicas) if j % 2 == k] for k in range(2)]
        final[2:] = lax.psum(tuple(final[2:]), "replica", axis_index_groups=groups)
    return tuple(final)


def solution(mesh):
    return jax.shard_map(
        local,
        mesh=mesh,
        in_specs=(
            P(("fsdp", "replica"), None),
            P(("fsdp", "replica"), None),
            P("fsdp"),
            P("fsdp"),
            P("fsdp", None),
            P("fsdp"),
            P("fsdp", None),
            P("fsdp"),
            P("fsdp"),
            P("fsdp"),
            P("fsdp", None),
            P("fsdp"),
            P("fsdp", None),
            P("fsdp"),
        ),
        out_specs=(
            P(("fsdp", "replica"), None),
            P(("fsdp", "replica"), None),
            P("fsdp"),
            P("fsdp"),
            P("fsdp", None),
            P("fsdp"),
            P("fsdp", None),
            P("fsdp"),
            P("fsdp"),
            P("fsdp"),
            P("fsdp", None),
            P("fsdp"),
            P("fsdp", None),
            P("fsdp"),
        ),
        check_vma=False,
    )
```
